32 devices in a mesh: ctx: 16 (over z, x, core), head: 2 (over y).
Axes of the slice: x: 2, y: 2, z: 4, core: 2. Of those that a mesh axis runs over, the one named last changes fastest.
Arguments:
- queries: bfloat16 [64, 2048], P(('ctx', 'head')), may hold values from -150 to 150
- new_block_keys: bfloat16 [64, 512], P(('ctx', 'head')), may hold values from -6 to 6
- new_block_values: bfloat16 [64, 512], P(('ctx', 'head')), may hold values from -6 to 6
- stored_keys: bfloat16 [7168, 512], P('ctx', 'head'), may hold values from -6 to 6
- stored_values: bfloat16 [7168, 512], P('ctx', 'head'), may hold values from -6 to 6
- stretch_start: int32 [1], replicated, may hold values from 3584 to 7168
- block_order: int32 [32], replicated, may hold values from 0 to 31, each once
Outputs:
- attended: bfloat16 [64, 2048], P(('ctx', 'head'))
The draws below stay inside these ranges and needn't reach their ends.
Inputs may be any that keep to these rules, and one draw needn't show every extreme that they name: `block_order`: each value appears once.
All inputs are finite; a program needn't handle non-finite values.
Results may differ from the reference program's by a relative error of at most 0.0049.
Values may be sent and summed in bfloat16 or wider, within the bound.
A program may use at most 128 MiB of HBM per device.

```python
import math
import jax
import jax.numpy as jnp
from jax import lax

QUERY_HEADS = 16
KEY_VALUE_HEADS = 4
HEAD_WIDTH = 128
Q_CTX = 4
BLOCK_TOKENS = 64
CACHED_SLOTS = 7168
N_CTX = 16


def cache_base(key):
    unscaled_scores = jax.random.normal(jax.random.fold_in(key, 7001), (CACHED_SLOTS, KEY_VALUE_HEADS * HEAD_WIDTH), jnp.float32)
    return jnp.clip(unscaled_scores, -6.0, 6.0)


def draw_stored_keys(key, part):
    base = cache_base(key)
    return base.astype(jnp.bfloat16)


def draw_queries(key, part):
    unscaled_scores = jax.random.normal(jax.random.fold_in(key, 7002), (BLOCK_TOKENS, QUERY_HEADS * HEAD_WIDTH), jnp.float32)
    base = jnp.clip(unscaled_scores, -6.0, 6.0)
    return base.astype(jnp.bfloat16)


def steps_of(stream_key, dims, shards, least, top_value):
    level = 1.0
    for position, shards_of in shards:
        heights = jax.random.uniform(jax.random.fold_in(jax.random.fold_in(stream_key, 6), position), (shards_of,), jnp.float32, least / len(shards), top_value / len(shards))
        level = level * jnp.repeat(jnp.exp(heights), dims[position] // shards_of).reshape((-1,) + (1,) * (len(dims) - 1 - position))
    return level


def centred(rng, shape, deviation, limit, pieces=(), kind=jnp.bfloat16):
    level = steps_of(rng, shape, pieces, -0.22, 0.18) if pieces else 1.0
    result = jax.random.normal(rng, shape, jnp.float32) * deviation * level
    return jnp.minimum(jnp.maximum(result, -limit), limit).astype(kind)


def setup_inputs(seed: int = 0) -> dict:
    splits = jax.random.split(jax.random.key(seed), 8)
    return {
        "queries": draw_queries(jax.random.fold_in(splits[7], 71), 0),
        "new_block_keys": centred(splits[1], (BLOCK_TOKENS, KEY_VALUE_HEADS * HEAD_WIDTH), 1.0, 6.0, ((0, 32),)),
        "new_block_values": centred(splits[2], (BLOCK_TOKENS, KEY_VALUE_HEADS * HEAD_WIDTH), 1.0, 6.0, ((0, 32),)),
        "stored_keys": draw_stored_keys(jax.random.fold_in(splits[7], 71), 0),
        "stored_values": centred(splits[4], (CACHED_SLOTS, KEY_VALUE_HEADS * HEAD_WIDTH), 1.0, 6.0, ((0, 16), (1, 2))),
        "stretch_start": jax.random.randint(splits[5], (1,), CACHED_SLOTS // 2, CACHED_SLOTS + 1).astype(jnp.int32),
        "block_order": jax.random.permutation(splits[6], 2 * N_CTX).astype(jnp.int32),
    }


NEG_FILL = -1e+30

def reference(queries, new_block_keys, new_block_values, stored_keys, stored_values, stretch_start, block_order):
    half_rows = Q_CTX // 2
    stretch_first = stretch_start[0]
    row_ids = jnp.arange(BLOCK_TOKENS, dtype=jnp.int32)
    query_pos = stretch_first + block_order[row_ids // half_rows] * half_rows + row_ids % half_rows
    cache_pos = jnp.arange(CACHED_SLOTS, dtype=jnp.int32)
    key_pos = jnp.concatenate([cache_pos, query_pos])
    usable = jnp.concatenate([cache_pos < stretch_first, jnp.ones((BLOCK_TOKENS,), dtype=bool)])
    query_group_width = QUERY_HEADS // KEY_VALUE_HEADS
    every_row = CACHED_SLOTS + BLOCK_TOKENS
    joined_keys = jnp.concatenate([stored_keys, new_block_keys], 0).astype(jnp.float32).reshape(every_row, KEY_VALUE_HEADS, HEAD_WIDTH)
    joined_values = jnp.concatenate([stored_values, new_block_values], 0).astype(jnp.float32).reshape(every_row, KEY_VALUE_HEADS, HEAD_WIDTH)
    score_scale = 1.0 / math.sqrt(HEAD_WIDTH)
    rows_of_block = math.gcd(BLOCK_TOKENS, 64)

    def one_block(block_index):
        start_row = block_index * rows_of_block
        query_row_block = lax.dynamic_slice_in_dim(queries, start_row, rows_of_block, 0).astype(jnp.float32)
        query_row_block = query_row_block.reshape(rows_of_block, KEY_VALUE_HEADS, query_group_width, HEAD_WIDTH)
        pos_q = lax.dynamic_slice_in_dim(query_pos, start_row, rows_of_block, 0)
        scores = jnp.einsum('bhgd,khd->bhgk', query_row_block, joined_keys) * score_scale
        allowed = usable[None, :] & (key_pos[None, :] <= pos_q[:, None])
        allowed = allowed[:, None, None, :]
        row_peak = lax.optimization_barrier(jnp.max(jnp.where(allowed, scores, NEG_FILL), axis=-1, keepdims=True))
        weights = jnp.where(allowed, jnp.exp(scores - row_peak), 0.0)
        totals = lax.optimization_barrier(jnp.sum(weights, axis=-1))
        rounded = lax.optimization_barrier(weights.astype(jnp.bfloat16)).astype(jnp.float32)
        mixed = jnp.einsum('bhgk,khd->bhgd', rounded, joined_values) / totals[..., None]
        return mixed.reshape(rows_of_block, QUERY_HEADS * HEAD_WIDTH).astype(jnp.bfloat16)
    blocks_out = lax.map(one_block, jnp.arange(BLOCK_TOKENS // rows_of_block, dtype=jnp.int32))
    return blocks_out.reshape(BLOCK_TOKENS, QUERY_HEADS * HEAD_WIDTH)
```

```python
import functools
import math

import jax
import jax.numpy as jnp
from jax import lax
from jax.experimental import pallas as pl
from jax.experimental.pallas import tpu as pltpu
from jax.sharding import PartitionSpec as P

QUERY_HEADS = 16
KEY_VALUE_HEADS = 4
HEAD_WIDTH = 128
SHARE = QUERY_HEADS // KEY_VALUE_HEADS
NEG_FILL = -1e30
FAR = 2**30
TILE = 16
STAT_ROWS = 2
SCALE = 1.0 / math.sqrt(HEAD_WIDTH)
SCALE2 = SCALE * math.log2(math.e)
MESH = pl.DeviceIdType.MESH
F32 = jnp.float32
BF16 = jnp.bfloat16


def each(first, count, body):
    if count - first <= 64:
        for step in range(first, count):
            body(step)
    else:
        lax.fori_loop(first, count, lambda step, _: body(step), None)


def chunk_of(count):
    return max(c for c in range(1, 33) if count % c == 0)


def kernel(
    n_ctx,
    n_head,
    stretch_ref,
    order_hbm,
    q_hbm,
    nk_hbm,
    nv_hbm,
    k_hbm,
    v_hbm,
    out_ref,
    order_ref,
    q_ref,
    nk_ref,
    nv_ref,
    qsend,
    qrecv,
    kbuf,
    vbuf,
    fresh,
    newbuf,
    osend,
    orecv,
    local_sem,
    q_send,
    q_recv,
    kv_send,
    kv_recv,
    o_sems,
):
    n = n_ctx * n_head
    rows = q_hbm.shape[0]
    cache, width = k_hbm.shape
    fan = width // HEAD_WIDTH
    lines = SHARE * rows
    half = rows * n_head // 2
    per_half = half // rows
    crew = fan * n_head
    old_keys = cache * fan
    total_keys = kbuf.shape[0]
    ctx = lax.axis_index("ctx")
    head = lax.axis_index("head")
    me = ctx * n_head + head
    core = lax.rem(ctx, fan)
    lead = ctx - core

    def place(slot):
        return (slot // n_head, lax.rem(slot, n_head))

    def columns(member):
        return pl.ds(pl.multiple_of(member * HEAD_WIDTH, HEAD_WIDTH), HEAD_WIDTH)

    own_rows = pl.ds(pl.multiple_of(core * cache, TILE), cache)
    loads = [
        pltpu.make_async_copy(source, target, local_sem.at[i])
        for i, (source, target) in enumerate(
            (
                (q_hbm, q_ref),
                (nk_hbm, nk_ref),
                (nv_hbm, nv_ref),
                (order_hbm, order_ref),
                (k_hbm.at[:, columns(core)], kbuf.at[own_rows]),
                (v_hbm.at[:, columns(core)], vbuf.at[own_rows]),
            )
        )
    ]
    barrier = pltpu.get_barrier_semaphore()

    def greet(step):
        pl.semaphore_signal(
            barrier, inc=1, device_id=place(lax.rem(me + step, n)), device_id_type=MESH
        )

    each(1, n, greet)
    for load in loads:
        load.start()

    for load in loads[:3]:
        load.wait()
    block = q_ref[...].astype(F32)
    for g in range(KEY_VALUE_HEADS):
        pieces = [
            block[:, (g * SHARE + i) * HEAD_WIDTH : (g * SHARE + i + 1) * HEAD_WIDTH]
            for i in range(SHARE)
        ]
        qsend[g] = jnp.concatenate(pieces, axis=0).astype(BF16)
    blank = jnp.zeros((TILE - rows, HEAD_WIDTH), F32)
    for t, ref in enumerate((nk_ref, nv_ref)):
        new = ref[...].astype(F32)
        for g in range(KEY_VALUE_HEADS):
            part = new[:, g * HEAD_WIDTH : (g + 1) * HEAD_WIDTH]
            fresh[g, t] = jnp.concatenate([part, blank], axis=0).astype(BF16)

    pl.semaphore_wait(barrier, n - 1)

    group_of_me = jnp.where(me >= crew, 1, 0) + jnp.where(me >= n // 2, 1, 0)

    def send_queries(step):
        to_ctx, to_head = place(lax.rem(me + n - step, n))
        pltpu.make_async_remote_copy(
            src_ref=qsend.at[to_head * fan + lax.rem(to_ctx, fan)],
            dst_ref=qrecv.at[me],
            send_sem=q_send.at[0],
            recv_sem=q_recv.at[group_of_me],
            device_id=(to_ctx, to_head),
            device_id_type=MESH,
        ).start()

    each(1, n, send_queries)

    swaps = []
    for step in range(1, fan):
        to = lax.rem(core + step, fan)
        for t, (source, buf) in enumerate(((k_hbm, kbuf), (v_hbm, vbuf))):
            swap = pltpu.make_async_remote_copy(
                src_ref=source.at[:, columns(to)],
                dst_ref=buf.at[own_rows],
                send_sem=kv_send.at[1 + 2 * (step - 1) + t],
                recv_sem=kv_recv.at[1 + 2 * (step - 1) + t],
                device_id=(lead + to, head),
                device_id_type=MESH,
            )
            swap.start()
            swaps.append(swap)
    seat = core * n_head + head
    for step in range(1, crew):
        to = lax.rem(seat + step, crew)
        to_core, to_head = place(to)
        pltpu.make_async_remote_copy(
            src_ref=fresh.at[to_head * fan + to_core],
            dst_ref=newbuf.at[seat],
            send_sem=kv_send.at[0],
            recv_sem=kv_recv.at[0],
            device_id=(lead + to_core, to_head),
            device_id_type=MESH,
        ).start()

    mine = head * fan + core
    qrecv[me] = qsend[mine]
    newbuf[seat] = fresh[mine]
    spare = total_keys - old_keys - TILE * crew
    if spare:
        for buf in (kbuf, vbuf):
            buf[total_keys - spare :] = jnp.zeros((spare, HEAD_WIDTH), BF16)

    for load in loads[3:]:
        load.wait()

    def start_of(slot):
        return order_ref[slot // per_half] * half + lax.rem(slot, per_half) * rows

    split = (old_keys // 128) * 128
    column = lax.broadcasted_iota(jnp.int32, (1, total_keys), 1)
    spot = lead * cache + column
    key_pos = jnp.where((column < old_keys) & (spot < stretch_ref[0]), -1, FAR)
    for j in range(crew):
        offset = column - (old_keys + TILE * j)
        pos = start_of(lead * n_head + j) + offset
        key_pos = jnp.where((offset >= 0) & (offset < rows), pos, key_pos)

    for swap in swaps:
        swap.wait()
    if crew > 1:
        others = newbuf.at[pl.ds(0, crew - 1)]
        news = pltpu.make_async_remote_copy(
            src_ref=others,
            dst_ref=others,
            send_sem=kv_send.at[0],
            recv_sem=kv_recv.at[0],
            device_id=(ctx, head),
            device_id_type=MESH,
        )
        news.wait()
    for t, buf in enumerate((kbuf, vbuf)):
        for j in range(crew):
            buf[old_keys + TILE * j : old_keys + TILE * (j + 1)] = newbuf[j, t]

    def arrived(first, count, index):
        def expect(slots):
            block = qrecv.at[pl.ds(first, slots)]
            pltpu.make_async_remote_copy(
                src_ref=block,
                dst_ref=block,
                send_sem=q_send.at[0],
                recv_sem=q_recv.at[index],
                device_id=(ctx, head),
                device_id_type=MESH,
            ).wait_recv()

        @pl.when(group_of_me == index)
        def _():
            expect(count - 1)

        @pl.when(group_of_me != index)
        def _():
            expect(count)

    def attend(first, group):
        size = group * lines
        q = qrecv[pl.ds(first, group)].astype(F32).reshape(size, HEAD_WIDTH).astype(BF16)
        scores = lax.dot_general(
            q, kbuf[...], (((1,), (1,)), ((), ())), preferred_element_type=F32
        )
        tail = total_keys - split
        query_pos = jnp.concatenate(
            [jnp.full((lines, tail), start_of(first + i), jnp.int32) for i in range(group)],
            axis=0,
        )
        query_pos = query_pos + lax.rem(
            lax.broadcasted_iota(jnp.int32, (size, tail), 0), rows
        )
        old = jnp.where(key_pos[:, :split] < 0, scores[:, :split], NEG_FILL)
        new = jnp.where(key_pos[:, split:] <= query_pos, scores[:, split:], NEG_FILL)
        scores = jnp.concatenate([old, new], axis=1)
        peak = jnp.max(scores, axis=1, keepdims=True)
        weights = jnp.exp2((scores - peak) * SCALE2)
        total = jnp.sum(weights, axis=1, keepdims=True)
        part = lax.dot_general(
            weights.astype(BF16),
            vbuf[...],
            (((1,), (0,)), ((), ())),
            preferred_element_type=F32,
        )
        part = part / total
        mass = peak * SCALE + jnp.log(total)
        high = mass.astype(BF16).astype(F32)
        rest = mass - high
        mid = rest.astype(BF16).astype(F32)
        low = rest - mid
        lane = lax.broadcasted_iota(jnp.int32, (size, HEAD_WIDTH), 1)
        line = lax.rem(lax.broadcasted_iota(jnp.int32, (size, HEAD_WIDTH), 0), lines)
        stat = jnp.where(lane < lines, high, jnp.where(lane < 2 * lines, mid, low))
        stat = jnp.where((lane < 3 * lines) & (lax.rem(lane, lines) == line), stat, 0.0)
        stat = jnp.sum(stat.reshape(group, lines, HEAD_WIDTH), axis=1, keepdims=True)
        osend[pl.ds(first, group), 0:lines] = part.reshape(group, lines, HEAD_WIDTH).astype(BF16)
        osend[pl.ds(first, group), lines : lines + STAT_ROWS] = jnp.broadcast_to(
            stat, (group, STAT_ROWS, HEAD_WIDTH)
        ).astype(BF16)

    def send_part(slot):
        @pl.when(slot != me)
        def _():
            pltpu.make_async_remote_copy(
                src_ref=osend.at[slot],
                dst_ref=orecv.at[me],
                send_sem=o_sems.at[0],
                recv_sem=o_sems.at[1],
                device_id=place(slot),
                device_id_type=MESH,
            ).start()

    for index, first, last in ((2, n // 2, n), (0, 0, crew), (1, crew, n // 2)):
        count = last - first
        if count == 0:
            continue
        arrived(first, count, index)
        group = chunk_of(count)
        each(0, count // group, lambda i: attend(first + i * group, group))
        if index == 0:
            for h in range(n_head):
                for c in range(fan):
                    send_part(c * n_head + h)
        else:
            each(0, count, lambda i: send_part(first + lax.rem(me + i, count)))

    orecv[me] = osend[me]
    q_all = qrecv.at[pl.ds(0, n - 1)]
    pltpu.make_async_remote_copy(
        src_ref=q_all,
        dst_ref=q_all,
        send_sem=q_send.at[0],
        recv_sem=q_recv.at[0],
        device_id=(ctx, head),
        device_id_type=MESH,
    ).wait_send()
    o_all = orecv.at[pl.ds(0, n - 1)]
    o_done = pltpu.make_async_remote_copy(
        src_ref=o_all,
        dst_ref=o_all,
        send_sem=o_sems.at[0],
        recv_sem=o_sems.at[1],
        device_id=(ctx, head),
        device_id_type=MESH,
    )
    o_done.wait_recv()

    lane = lax.broadcasted_iota(jnp.int32, (lines, HEAD_WIDTH), 1)
    line = lax.broadcasted_iota(jnp.int32, (lines, HEAD_WIDTH), 0)
    diagonal = (lane < 3 * lines) & (lax.rem(lane, lines) == line)
    shape = (n_ctx // fan, crew)
    parts = orecv[:, 0:lines].astype(F32).reshape(*shape, lines, HEAD_WIDTH)
    stats = orecv[:, lines : lines + STAT_ROWS].astype(F32)
    stats = stats.reshape(*shape, STAT_ROWS, HEAD_WIDTH)
    for j in range(crew):
        c, h = divmod(j, n_head)
        spread = jnp.where(diagonal[None], stats[:, j, 0:1], 0.0)
        mass = jnp.sum(spread, axis=2, keepdims=True)
        top = jnp.max(mass, axis=0, keepdims=True)
        share = jnp.exp(mass - top)
        result = jnp.sum(share * parts[:, j], axis=0) / jnp.sum(share, axis=0)
        for i in range(SHARE):
            at = ((h * fan + c) * SHARE + i) * HEAD_WIDTH
            out_ref[:, at : at + HEAD_WIDTH] = result[i * rows : (i + 1) * rows].astype(BF16)
    o_done.wait_send()


def on_device(
    n_ctx,
    n_head,
    queries,
    new_block_keys,
    new_block_values,
    stored_keys,
    stored_values,
    stretch_start,
    block_order,
):
    n = n_ctx * n_head
    rows = queries.shape[0]
    cache, width = stored_keys.shape
    fan = width // HEAD_WIDTH
    crew = fan * n_head
    lines = SHARE * rows
    total_keys = cache * fan + TILE * crew
    total_keys = (total_keys + 127) // 128 * 128
    dma = pltpu.SemaphoreType.DMA
    return pl.pallas_call(
        functools.partial(kernel, n_ctx, n_head),
        out_shape=jax.ShapeDtypeStruct(queries.shape, BF16),
        in_specs=[pl.BlockSpec(memory_space=pltpu.SMEM)]
        + [pl.BlockSpec(memory_space=pltpu.HBM)] * 6,
        out_specs=pl.BlockSpec(memory_space=pltpu.VMEM),
        scratch_shapes=[
            pltpu.SMEM(block_order.shape, jnp.int32),
            pltpu.VMEM(queries.shape, BF16),
            pltpu.VMEM(new_block_keys.shape, BF16),
            pltpu.VMEM(new_block_values.shape, BF16),
            pltpu.VMEM((KEY_VALUE_HEADS, lines, HEAD_WIDTH), BF16),
            pltpu.VMEM((n, lines, HEAD_WIDTH), BF16),
            pltpu.VMEM((total_keys, HEAD_WIDTH), BF16),
            pltpu.VMEM((total_keys, HEAD_WIDTH), BF16),
            pltpu.VMEM((KEY_VALUE_HEADS, 2, TILE, HEAD_WIDTH), BF16),
            pltpu.VMEM((crew, 2, TILE, HEAD_WIDTH), BF16),
            pltpu.VMEM((n, lines + STAT_ROWS, HEAD_WIDTH), BF16),
            pltpu.VMEM((n, lines + STAT_ROWS, HEAD_WIDTH), BF16),
            dma((6,)),
            dma((1,)),
            dma((3,)),
            dma((2 * fan - 1,)),
            dma((2 * fan - 1,)),
            dma((2,)),
        ],
        compiler_params=pltpu.CompilerParams(
            collective_id=0, has_side_effects=True, vmem_limit_bytes=48 * 1024 * 1024
        ),
    )(
        stretch_start,
        *[
            pltpu.with_memory_space_constraint(x, pltpu.HBM)
            for x in (
                block_order,
                queries,
                new_block_keys,
                new_block_values,
                stored_keys,
                stored_values,
            )
        ],
    )


def solution(mesh):
    return jax.shard_map(
        functools.partial(on_device, mesh.shape["ctx"], mesh.shape["head"]),
        mesh=mesh,
        in_specs=(
            P(("ctx", "head"), None),
            P(("ctx", "head"), None),
            P(("ctx", "head"), None),
            P("ctx", "head"),
            P("ctx", "head"),
            P(),
            P(),
        ),
        out_specs=P(("ctx", "head"), None),
        check_vma=False,
    )
```

```python
import functools
import math

import jax
import jax.numpy as jnp
from jax import lax
from jax.experimental import pallas as pl
from jax.experimental.pallas import tpu as pltpu
from jax.sharding import PartitionSpec as P

QUERY_HEADS = 16
KEY_VALUE_HEADS = 4
HEAD_WIDTH = 128
SHARE = QUERY_HEADS // KEY_VALUE_HEADS
NEG_FILL = -1e30
FAR = 2**30
TILE = 16
STAT_ROWS = 2
SCALE = 1.0 / math.sqrt(HEAD_WIDTH)
SCALE2 = SCALE * math.log2(math.e)
MESH = pl.DeviceIdType.MESH
F32 = jnp.float32
BF16 = jnp.bfloat16


def each(first, count, body):
    if count - first <= 64:
        for step in range(first, count):
            body(step)
    else:
        lax.fori_loop(first, count, lambda step, _: body(step), None)


def chunk_of(count):
    return max(c for c in range(1, 33) if count % c == 0)


def kernel(
    n_ctx,
    n_head,
    stretch_ref,
    order_hbm,
    q_hbm,
    nk_hbm,
    nv_hbm,
    k_hbm,
    v_hbm,
    out_ref,
    order_ref,
    stage,
    qsend,
    carry,
    qrecv,
    kv,
    fresh,
    newbuf,
    osend,
    orecv,
    local_sem,
    q_send,
    q_recv,
    kv_send,
    kv_recv,
    o_sems,
):
    n = n_ctx * n_head
    rows = q_hbm.shape[0]
    cache, width = k_hbm.shape
    fan = width // HEAD_WIDTH
    lines = SHARE * rows
    half = rows * n_head // 2
    per_half = half // rows
    crew = fan * n_head
    plane = n_ctx // 4
    early = plane * n_head
    old_keys = cache * fan
    total_keys = kv.shape[1]
    ctx = lax.axis_index("ctx")
    head = lax.axis_index("head")
    me = ctx * n_head + head
    core = lax.rem(ctx, fan)
    lead = ctx - core
    seat = core * n_head + head
    mine = head * fan + core
    is_early = ctx < plane
    is_relay = (ctx >= plane) & (ctx < 2 * plane)

    def place(slot):
        return (slot // n_head, lax.rem(slot, n_head))

    def columns(member):
        return pl.ds(pl.multiple_of(member * HEAD_WIDTH, HEAD_WIDTH), HEAD_WIDTH)

    def remote(source, target, send, recv, to):
        return pltpu.make_async_remote_copy(
            src_ref=source,
            dst_ref=target,
            send_sem=send,
            recv_sem=recv,
            device_id=to,
            device_id_type=MESH,
        )

    barrier = pltpu.get_barrier_semaphore()

    def greet(slot):
        @pl.when(slot != me)
        def _():
            pl.semaphore_signal(
                barrier, inc=1, device_id=place(slot), device_id_type=MESH
            )

    each(0, early, lambda i: greet(early + lax.rem(me + i, early)))
    each(0, n - 2 * early, lambda i: greet(2 * early + lax.rem(me + i, n - 2 * early)))

    @pl.when(is_early)
    def _():
        for step in range(1, crew):
            c, h = place(lax.rem(seat + step, crew))
            pl.semaphore_signal(
                barrier, inc=1, device_id=(lead + c, h), device_id_type=MESH
            )

    @pl.when(is_relay)
    def _():
        pl.semaphore_signal(
            barrier, inc=1, device_id=(ctx - plane, head), device_id_type=MESH
        )

    own_rows = pl.ds(pl.multiple_of(core * cache, TILE), cache)
    q_width = q_hbm.shape[1]
    new_width = nk_hbm.shape[1]
    at = 0
    for source in (q_hbm, nk_hbm, nv_hbm):
        wide = source.shape[1]
        pltpu.make_async_copy(source, stage.at[:, at : at + wide], local_sem.at[0]).start()
        at += wide
    order_load = pltpu.make_async_copy(order_hbm, order_ref, local_sem.at[1])
    order_load.start()
    for t, source in enumerate((k_hbm, v_hbm)):
        pltpu.make_async_copy(
            source.at[:, columns(core)], kv.at[t, own_rows], local_sem.at[2]
        ).start()

    pltpu.make_async_copy(stage, stage, local_sem.at[0]).wait()
    block = stage[:, :q_width].astype(F32)
    for g in range(KEY_VALUE_HEADS):
        pieces = [
            block[:, (g * SHARE + i) * HEAD_WIDTH : (g * SHARE + i + 1) * HEAD_WIDTH]
            for i in range(SHARE)
        ]
        qsend[g] = jnp.concatenate(pieces, axis=0).astype(BF16)
    blank = jnp.zeros((TILE - rows, HEAD_WIDTH), F32)
    for t in range(2):
        new = stage[:, q_width + t * new_width : q_width + (t + 1) * new_width].astype(F32)
        for g in range(KEY_VALUE_HEADS):
            part = new[:, g * HEAD_WIDTH : (g + 1) * HEAD_WIDTH]
            fresh[g, t] = jnp.concatenate([part, blank], axis=0).astype(BF16)

    @pl.when(is_early)
    def _():
        pl.semaphore_wait(barrier, crew)

    @pl.when(jnp.logical_not(is_early))
    def _():
        pl.semaphore_wait(barrier, n - 1)

    for step in range(1, fan):
        to = lax.rem(core + step, fan)
        for t, source in enumerate((k_hbm, v_hbm)):
            remote(
                source.at[:, columns(to)],
                kv.at[t, own_rows],
                kv_send.at[0],
                kv_recv.at[0],
                (lead + to, head),
            ).start()
    for step in range(1, crew):
        to_core, to_head = place(lax.rem(seat + step, crew))
        remote(
            fresh.at[to_head * fan + to_core],
            newbuf.at[seat],
            kv_send.at[1],
            kv_recv.at[1],
            (lead + to_core, to_head),
        ).start()

    group_of_me = jnp.where(me >= early, 1, 0) + jnp.where(me >= 2 * early, 1, 0)

    def head_of(slot):
        c, h = place(slot)
        return h * fan + lax.rem(c, fan)

    @pl.when(is_early)
    def _():
        remote(qsend, carry, q_send.at[0], q_recv.at[3], (ctx + plane, head)).start()

    @pl.when(is_relay)
    def _():
        remote(qsend, carry, q_send.at[0], q_recv.at[3], (ctx, head)).wait_recv()
        origin = me - early

        def pass_on(step):
            to = lax.rem(me + n - step, n)

            @pl.when(to != origin)
            def _():
                remote(
                    carry.at[head_of(to)],
                    qrecv.at[origin],
                    q_send.at[1],
                    q_recv.at[0],
                    place(to),
                ).start()

        each(1, n, pass_on)
        qrecv[origin] = carry[mine]

    def send_queries(step):
        to = lax.rem(me + n - step, n)
        remote(
            qsend.at[head_of(to)],
            qrecv.at[me],
            q_send.at[0],
            q_recv.at[group_of_me],
            place(to),
        ).start()

    @pl.when(jnp.logical_not(is_early))
    def _():
        each(1, n, send_queries)

    qrecv[me] = qsend[mine]
    newbuf[seat] = fresh[mine]
    spare = total_keys - old_keys - TILE * crew
    if spare:
        for t in range(2):
            kv[t, total_keys - spare :] = jnp.zeros((spare, HEAD_WIDTH), BF16)

    order_load.wait()
    own = kv.at[:, own_rows]
    pltpu.make_async_copy(own, own, local_sem.at[2]).wait()

    def start_of(slot):
        return order_ref[slot // per_half] * half + lax.rem(slot, per_half) * rows

    split = (old_keys // 128) * 128
    column = lax.broadcasted_iota(jnp.int32, (1, total_keys), 1)
    spot = lead * cache + column
    key_pos = jnp.where((column < old_keys) & (spot < stretch_ref[0]), -1, FAR)
    for j in range(crew):
        offset = column - (old_keys + TILE * j)
        pos = start_of(lead * n_head + j) + offset
        key_pos = jnp.where((offset >= 0) & (offset < rows), pos, key_pos)

    here = (ctx, head)
    if fan > 1:
        others = kv.at[:, pl.ds(0, cache * (fan - 1))]
        remote(others, others, kv_send.at[0], kv_recv.at[0], here).wait()
    if crew > 1:
        others = newbuf.at[pl.ds(0, crew - 1)]
        remote(others, others, kv_send.at[1], kv_recv.at[1], here).wait()
    for t in range(2):
        for j in range(crew):
            kv[t, old_keys + TILE * j : old_keys + TILE * (j + 1)] = newbuf[j, t]

    def arrived(first, count, index):
        def expect(slots):
            block = qrecv.at[pl.ds(first, slots)]
            remote(block, block, q_send.at[0], q_recv.at[index], here).wait_recv()

        less = (group_of_me == index) | ((index == 0) & is_relay)

        @pl.when(less)
        def _():
            expect(count - 1)

        @pl.when(jnp.logical_not(less))
        def _():
            expect(count)

    def attend(first, group):
        size = group * lines
        q = qrecv[pl.ds(first, group)].astype(F32).reshape(size, HEAD_WIDTH).astype(BF16)
        scores = lax.dot_general(
            q, kv[0], (((1,), (1,)), ((), ())), preferred_element_type=F32
        )
        tail = total_keys - split
        query_pos = jnp.concatenate(
            [jnp.full((lines, tail), start_of(first + i), jnp.int32) for i in range(group)],
            axis=0,
        )
        query_pos = query_pos + lax.rem(
            lax.broadcasted_iota(jnp.int32, (size, tail), 0), rows
        )
        old = jnp.where(key_pos[:, :split] < 0, scores[:, :split], NEG_FILL)
        new = jnp.where(key_pos[:, split:] <= query_pos, scores[:, split:], NEG_FILL)
        scores = jnp.concatenate([old, new], axis=1)
        peak = jnp.max(scores, axis=1, keepdims=True)
        weights = jnp.exp2((scores - peak) * SCALE2)
        total = jnp.sum(weights, axis=1, keepdims=True)
        part = lax.dot_general(
            weights.astype(BF16),
            kv[1],
            (((1,), (0,)), ((), ())),
            preferred_element_type=F32,
        )
        part = part / total
        mass = peak * SCALE + jnp.log(total)
        high = mass.astype(BF16).astype(F32)
        rest = mass - high
        mid = rest.astype(BF16).astype(F32)
        low = rest - mid
        lane = lax.broadcasted_iota(jnp.int32, (size, HEAD_WIDTH), 1)
        line = lax.rem(lax.broadcasted_iota(jnp.int32, (size, HEAD_WIDTH), 0), lines)
        stat = jnp.where(lane < lines, high, jnp.where(lane < 2 * lines, mid, low))
        stat = jnp.where((lane < 3 * lines) & (lax.rem(lane, lines) == line), stat, 0.0)
        stat = jnp.sum(stat.reshape(group, lines, HEAD_WIDTH), axis=1, keepdims=True)
        osend[pl.ds(first, group), 0:lines] = part.reshape(group, lines, HEAD_WIDTH).astype(BF16)
        osend[pl.ds(first, group), lines : lines + STAT_ROWS] = jnp.broadcast_to(
            stat, (group, STAT_ROWS, HEAD_WIDTH)
        ).astype(BF16)

    def send_part(slot):
        @pl.when(slot != me)
        def _():
            remote(
                osend.at[slot], orecv.at[me], o_sems.at[0], o_sems.at[1], place(slot)
            ).start()

    for index, first, last in ((2, 2 * early, n), (0, 0, early), (1, early, 2 * early)):
        count = last - first
        arrived(first, count, index)
        group = chunk_of(count)
        each(0, count // group, lambda i: attend(first + i * group, group))
        if index == 0:
            each(first, last, send_part)
        else:
            each(0, count, lambda i: send_part(first + lax.rem(me + i, count)))

    orecv[me] = osend[me]

    @pl.when(is_early)
    def _():
        remote(qsend, carry, q_send.at[0], q_recv.at[3], here).wait_send()

    @pl.when(jnp.logical_not(is_early))
    def _():
        block = qrecv.at[pl.ds(0, n - 1)]
        remote(block, block, q_send.at[0], q_recv.at[0], here).wait_send()

    @pl.when(is_relay)
    def _():
        block = qrecv.at[pl.ds(0, n - 2)]
        remote(block, block, q_send.at[1], q_recv.at[0], here).wait_send()

    o_all = orecv.at[pl.ds(0, n - 1)]
    o_done = remote(o_all, o_all, o_sems.at[0], o_sems.at[1], here)
    o_done.wait_recv()

    lane = lax.broadcasted_iota(jnp.int32, (lines, HEAD_WIDTH), 1)
    line = lax.broadcasted_iota(jnp.int32, (lines, HEAD_WIDTH), 0)
    diagonal = (lane < 3 * lines) & (lax.rem(lane, lines) == line)
    shape = (n_ctx // fan, crew)
    parts = orecv[:, 0:lines].astype(F32).reshape(*shape, lines, HEAD_WIDTH)
    stats = orecv[:, lines : lines + STAT_ROWS].astype(F32)
    stats = stats.reshape(*shape, STAT_ROWS, HEAD_WIDTH)
    for j in range(crew):
        c, h = divmod(j, n_head)
        spread = jnp.where(diagonal[None], stats[:, j, 0:1], 0.0)
        mass = jnp.sum(spread, axis=2, keepdims=True)
        top = jnp.max(mass, axis=0, keepdims=True)
        share = jnp.exp(mass - top)
        result = jnp.sum(share * parts[:, j], axis=0) / jnp.sum(share, axis=0)
        for i in range(SHARE):
            at = ((h * fan + c) * SHARE + i) * HEAD_WIDTH
            out_ref[:, at : at + HEAD_WIDTH] = result[i * rows : (i + 1) * rows].astype(BF16)
    o_done.wait_send()


def on_device(
    n_ctx,
    n_head,
    queries,
    new_block_keys,
    new_block_values,
    stored_keys,
    stored_values,
    stretch_start,
    block_order,
):
    n = n_ctx * n_head
    rows = queries.shape[0]
    cache, width = stored_keys.shape
    fan = width // HEAD_WIDTH
    crew = fan * n_head
    lines = SHARE * rows
    total_keys = cache * fan + TILE * crew
    total_keys = (total_keys + 127) // 128 * 128
    dma = pltpu.SemaphoreType.DMA
    return pl.pallas_call(
        functools.partial(kernel, n_ctx, n_head),
        out_shape=jax.ShapeDtypeStruct(queries.shape, BF16),
        in_specs=[pl.BlockSpec(memory_space=pltpu.SMEM)]
        + [pl.BlockSpec(memory_space=pltpu.HBM)] * 6,
        out_specs=pl.BlockSpec(memory_space=pltpu.VMEM),
        scratch_shapes=[
            pltpu.SMEM(block_order.shape, jnp.int32),
            pltpu.VMEM((rows, queries.shape[1] + 2 * new_block_keys.shape[1]), BF16),
            pltpu.VMEM((KEY_VALUE_HEADS, lines, HEAD_WIDTH), BF16),
            pltpu.VMEM((KEY_VALUE_HEADS, lines, HEAD_WIDTH), BF16),
            pltpu.VMEM((n, lines, HEAD_WIDTH), BF16),
            pltpu.VMEM((2, total_keys, HEAD_WIDTH), BF16),
            pltpu.VMEM((KEY_VALUE_HEADS, 2, TILE, HEAD_WIDTH), BF16),
            pltpu.VMEM((crew, 2, TILE, HEAD_WIDTH), BF16),
            pltpu.VMEM((n, lines + STAT_ROWS, HEAD_WIDTH), BF16),
            pltpu.VMEM((n, lines + STAT_ROWS, HEAD_WIDTH), BF16),
            dma((3,)),
            dma((2,)),
            dma((4,)),
            dma((2,)),
            dma((2,)),
            dma((2,)),
        ],
        compiler_params=pltpu.CompilerParams(
            collective_id=0, has_side_effects=True, vmem_limit_bytes=48 * 1024 * 1024
        ),
    )(
        stretch_start,
        *[
            pltpu.with_memory_space_constraint(x, pltpu.HBM)
            for x in (
                block_order,
                queries,
                new_block_keys,
                new_block_values,
                stored_keys,
                stored_values,
            )
        ],
    )


def solution(mesh):
    return jax.shard_map(
        functools.partial(on_device, mesh.shape["ctx"], mesh.shape["head"]),
        mesh=mesh,
        in_specs=(
            P(("ctx", "head"), None),
            P(("ctx", "head"), None),
            P(("ctx", "head"), None),
            P("ctx", "head"),
            P("ctx", "head"),
            P(),
            P(),
        ),
        out_specs=P(("ctx", "head"), None),
        check_vma=False,
    )
```

```python
import functools
import math

import jax
import jax.numpy as jnp
from jax import lax
from jax.experimental import pallas as pl
from jax.experimental.pallas import tpu as pltpu
from jax.sharding import PartitionSpec as P

QUERY_HEADS = 16
HEAD_WIDTH = 128
NEG_FILL = -1e30
FAR = 2**30
TILE = 16
PAIR = 2
STAT_ROWS = 2
SCALE = 1.0 / math.sqrt(HEAD_WIDTH)
SCALE2 = SCALE * math.log2(math.e)
MESH = pl.DeviceIdType.MESH
F32 = jnp.float32
BF16 = jnp.bfloat16


def each(first, count, body):
    if count - first <= 64:
        for step in range(first, count):
            body(step)
    else:
        lax.fori_loop(first, count, lambda step, _: body(step), None)


def chunk_of(count):
    return max(c for c in range(1, 33) if count % c == 0)


def kernel(
    n_ctx,
    n_head,
    stretch_ref,
    order_hbm,
    q_hbm,
    nk_hbm,
    nv_hbm,
    k_hbm,
    v_hbm,
    out_ref,
    order_ref,
    stage,
    qsend,
    carry,
    qrecv,
    kv,
    fresh,
    newbuf,
    osend,
    orecv,
    local_sem,
    q_send,
    q_recv,
    kv_send,
    kv_recv,
    o_sems,
):
    n = n_ctx * n_head
    rows = q_hbm.shape[0]
    cache, width = k_hbm.shape
    kv_heads = width // HEAD_WIDTH
    heads = QUERY_HEADS // n_head
    lines = heads * rows
    kv_lines = lines // kv_heads
    half = rows * n_head // 2
    per_half = half // rows
    crew = PAIR * n_head
    servers = n // 2
    plane = n_ctx // 4
    early = plane * n_head
    old_keys = cache * PAIR
    total_keys = kv.shape[1]
    ctx = lax.axis_index("ctx")
    head = lax.axis_index("head")
    me = ctx * n_head + head
    core = lax.rem(ctx, PAIR)
    lead = ctx - core
    seat = core * n_head + head
    desk = (ctx // PAIR) * n_head + head
    spot = lax.rem(me, servers)
    is_odd = core == 1
    is_low = ctx < 2 * plane
    is_early = ctx < plane
    is_relay = jnp.logical_not(is_early) & is_low
    own = jnp.where(is_low, core, 1 - core) == 1
    first_client = jnp.where(is_odd, 0, servers)

    def place(slot):
        return (slot // n_head, lax.rem(slot, n_head))

    def server_at(index):
        pair, h = place(index)
        return (pair * PAIR + jnp.where(is_low, 1, 0), h)

    def remote(source, target, send, recv, to):
        return pltpu.make_async_remote_copy(
            src_ref=source,
            dst_ref=target,
            send_sem=send,
            recv_sem=recv,
            device_id=to,
            device_id_type=MESH,
        )

    barrier = pltpu.get_barrier_semaphore()

    def signal(to):
        pl.semaphore_signal(barrier, inc=1, device_id=to, device_id_type=MESH)

    def greet(slot):
        @pl.when(slot != me)
        def _():
            signal(place(slot))

    @pl.when(is_odd)
    def _():
        each(0, early, lambda i: greet(early + lax.rem(me + i, early)))

    @pl.when(jnp.logical_not(is_odd))
    def _():
        each(0, servers, lambda i: greet(servers + lax.rem(me + i, servers)))

    @pl.when(is_relay)
    def _():
        signal((ctx - plane, head))

    for step in range(1, crew):
        c, h = place(lax.rem(seat + step, crew))
        signal((lead + c, h))

    own_rows = pl.ds(pl.multiple_of(core * cache, TILE), cache)
    q_width = q_hbm.shape[1]
    new_width = nk_hbm.shape[1]
    at = 0
    for source in (q_hbm, nk_hbm, nv_hbm):
        wide = source.shape[1]
        pltpu.make_async_copy(source, stage.at[:, at : at + wide], local_sem.at[0]).start()
        at += wide
    order_load = pltpu.make_async_copy(order_hbm, order_ref, local_sem.at[1])
    order_load.start()
    for t, source in enumerate((k_hbm, v_hbm)):
        pltpu.make_async_copy(source, kv.at[t, own_rows], local_sem.at[2]).start()

    pltpu.make_async_copy(stage, stage, local_sem.at[0]).wait()
    block = stage[:, :q_width].astype(F32)
    for h in range(n_head):
        pieces = [
            block[:, (h * heads + i) * HEAD_WIDTH : (h * heads + i + 1) * HEAD_WIDTH]
            for i in range(heads)
        ]
        qsend[h] = jnp.concatenate(pieces, axis=0).astype(BF16)
    blank = jnp.zeros((TILE - rows, width), F32)
    for t in range(2):
        new = stage[:, q_width + t * new_width : q_width + (t + 1) * new_width].astype(F32)
        for h in range(n_head):
            part = new[:, h * width : (h + 1) * width]
            fresh[h, t] = jnp.concatenate([part, blank], axis=0).astype(BF16)

    @pl.when(is_early)
    def _():
        pl.semaphore_wait(barrier, crew)

    @pl.when(jnp.logical_not(is_early) & own)
    def _():
        pl.semaphore_wait(barrier, servers - 1 + crew - 1)

    @pl.when(jnp.logical_not(is_early | own))
    def _():
        pl.semaphore_wait(barrier, servers + crew - 1)

    for t, source in enumerate((k_hbm, v_hbm)):
        remote(
            source, kv.at[t, own_rows], kv_send.at[0], kv_recv.at[0], (lead + 1 - core, head)
        ).start()
    for step in range(1, crew):
        to_core, to_head = place(lax.rem(seat + step, crew))
        remote(
            fresh.at[to_head],
            newbuf.at[seat],
            kv_send.at[1],
            kv_recv.at[1],
            (lead + to_core, to_head),
        ).start()

    wave = jnp.where(spot >= early, 1, 0)

    @pl.when(is_early)
    def _():
        remote(qsend, carry, q_send.at[0], q_recv.at[2], (ctx + plane, head)).start()

    @pl.when(is_relay)
    def _():
        remote(qsend, carry, q_send.at[0], q_recv.at[2], (ctx, head)).wait_recv()
        origin = me - early
        origin_desk = desk - early // PAIR

        def pass_on(step):
            to = servers - 1 - step

            @pl.when(jnp.logical_not(is_odd & ((to == origin_desk) | (to == desk))))
            def _():
                to_ctx, to_head = server_at(to)
                remote(
                    carry.at[to_head],
                    qrecv.at[origin],
                    q_send.at[1],
                    q_recv.at[0],
                    (to_ctx, to_head),
                ).start()

        each(0, servers, pass_on)

        @pl.when(is_odd)
        def _():
            qrecv[origin] = carry[head]

    def send_queries(step):
        to = lax.rem(desk + servers - step, servers)

        @pl.when(jnp.logical_not(own & (to == desk)))
        def _():
            to_ctx, to_head = server_at(to)
            remote(
                qsend.at[to_head],
                qrecv.at[spot],
                q_send.at[0],
                q_recv.at[wave],
                (to_ctx, to_head),
            ).start()

    @pl.when(jnp.logical_not(is_early))
    def _():
        each(1, servers + 1, send_queries)

    @pl.when(own)
    def _():
        qrecv[spot] = qsend[head]

    newbuf[seat] = fresh[head]
    spare = total_keys - old_keys - TILE * crew
    if spare:
        for t in range(2):
            kv[t, total_keys - spare :] = jnp.zeros((spare, width), BF16)

    order_load.wait()
    loaded = kv.at[:, own_rows]
    pltpu.make_async_copy(loaded, loaded, local_sem.at[2]).wait()

    def start_of(slot):
        return order_ref[slot // per_half] * half + lax.rem(slot, per_half) * rows

    split = (old_keys // 128) * 128
    column = lax.broadcasted_iota(jnp.int32, (1, total_keys), 1)
    cached = (column < old_keys) & (column + lead * cache < stretch_ref[0])
    key_pos = jnp.where(cached, -1, FAR)
    for j in range(crew):
        offset = column - (old_keys + TILE * j)
        pos = start_of(lead * n_head + j) + offset
        key_pos = jnp.where((offset >= 0) & (offset < rows), pos, key_pos)

    here = (ctx, head)
    remote(loaded, loaded, kv_send.at[0], kv_recv.at[0], here).wait()
    others = newbuf.at[pl.ds(0, crew - 1)]
    remote(others, others, kv_send.at[1], kv_recv.at[1], here).wait()
    for t in range(2):
        for j in range(crew):
            kv[t, old_keys + TILE * j : old_keys + TILE * (j + 1)] = newbuf[j, t]

    def expect(index, less, count):
        def wait_for(slots):
            block = qrecv.at[pl.ds(0, slots)]
            remote(block, block, q_send.at[0], q_recv.at[index], here).wait_recv()

        @pl.when(less)
        def _():
            wait_for(count - 1)

        @pl.when(jnp.logical_not(less))
        def _():
            wait_for(count)

    def attend(first, group):
        size = group * kv_lines
        block = qrecv[pl.ds(first, group)].astype(F32)
        tail = total_keys - split
        query_pos = jnp.concatenate(
            [
                jnp.full((kv_lines, tail), start_of(first_client + first + i), jnp.int32)
                for i in range(group)
            ],
            axis=0,
        )
        query_pos = query_pos + lax.rem(
            lax.broadcasted_iota(jnp.int32, (size, tail), 0), rows
        )
        lane = lax.broadcasted_iota(jnp.int32, (size, HEAD_WIDTH), 1)
        line = lax.rem(lax.broadcasted_iota(jnp.int32, (size, HEAD_WIDTH), 0), kv_lines)
        results = []
        stats = 0.0
        for g in range(kv_heads):
            q = block[:, g * kv_lines : (g + 1) * kv_lines]
            q = q.reshape(size, HEAD_WIDTH).astype(BF16)
            wide = slice(g * HEAD_WIDTH, (g + 1) * HEAD_WIDTH)
            scores = lax.dot_general(
                q, kv[0, :, wide], (((1,), (1,)), ((), ())), preferred_element_type=F32
            )
            old = jnp.where(key_pos[:, :split] < 0, scores[:, :split], NEG_FILL)
            new = jnp.where(key_pos[:, split:] <= query_pos, scores[:, split:], NEG_FILL)
            scores = jnp.concatenate([old, new], axis=1)
            peak = jnp.max(scores, axis=1, keepdims=True)
            weights = jnp.exp2((scores - peak) * SCALE2)
            total = jnp.sum(weights, axis=1, keepdims=True)
            part = lax.dot_general(
                weights.astype(BF16),
                kv[1, :, wide],
                (((1,), (0,)), ((), ())),
                preferred_element_type=F32,
            )
            results.append((part / total).reshape(group, kv_lines, HEAD_WIDTH))
            mass = peak * SCALE + jnp.log(total)
            high = mass.astype(BF16).astype(F32)
            rest = mass - high
            mid = rest.astype(BF16).astype(F32)
            low = rest - mid
            stat = jnp.where(lane < lines, high, jnp.where(lane < 2 * lines, mid, low))
            mark = (lane < 3 * lines) & (lax.rem(lane, lines) == line + g * kv_lines)
            stat = jnp.where(mark, stat, 0.0).reshape(group, kv_lines, HEAD_WIDTH)
            stats = stats + jnp.sum(stat, axis=1, keepdims=True)
        osend[pl.ds(first, group), 0:lines] = jnp.concatenate(results, axis=1).astype(BF16)
        osend[pl.ds(first, group), lines : lines + STAT_ROWS] = jnp.broadcast_to(
            stats, (group, STAT_ROWS, HEAD_WIDTH)
        ).astype(BF16)

    def send_part(index):
        slot = first_client + index

        @pl.when(slot != me)
        def _():
            remote(
                osend.at[index], orecv.at[desk], o_sems.at[0], o_sems.at[1], place(slot)
            ).start()

    for index, first, last in ((0, 0, early), (1, early, servers)):
        less = own & (wave == index)
        if index == 0:
            less = less | (own & is_relay)
        count = last - first
        expect(index, less, count)
        group = chunk_of(count)
        each(0, count // group, lambda i: attend(first + i * group, group))
        each(first, last, send_part)

    @pl.when(own)
    def _():
        orecv[desk] = osend[spot]

    def sent(sem, blocks):
        block = qrecv.at[pl.ds(0, blocks)]
        remote(block, block, sem, q_recv.at[0], here).wait_send()

    @pl.when(is_early)
    def _():
        sent(q_send.at[0], n_head)

    @pl.when(jnp.logical_not(is_early) & own)
    def _():
        sent(q_send.at[0], servers - 1)

    @pl.when(jnp.logical_not(is_early | own))
    def _():
        sent(q_send.at[0], servers)

    @pl.when(is_relay & is_odd)
    def _():
        sent(q_send.at[1], servers - 2)

    @pl.when(is_relay & jnp.logical_not(is_odd))
    def _():
        sent(q_send.at[1], servers)

    def answers(count):
        block = orecv.at[pl.ds(0, count)]
        return remote(block, block, o_sems.at[0], o_sems.at[1], here)

    @pl.when(own)
    def _():
        answers(servers - 1).wait_recv()

    @pl.when(jnp.logical_not(own))
    def _():
        answers(servers).wait_recv()

    lane = lax.broadcasted_iota(jnp.int32, (lines, HEAD_WIDTH), 1)
    line = lax.broadcasted_iota(jnp.int32, (lines, HEAD_WIDTH), 0)
    diagonal = (lane < 3 * lines) & (lax.rem(lane, lines) == line)
    shape = (n_ctx // PAIR, n_head)
    parts = orecv[:, 0:lines].astype(F32).reshape(*shape, lines, HEAD_WIDTH)
    stats = orecv[:, lines : lines + STAT_ROWS].astype(F32)
    stats = stats.reshape(*shape, STAT_ROWS, HEAD_WIDTH)
    for h in range(n_head):
        spread = jnp.where(diagonal[None], stats[:, h, 0:1], 0.0)
        mass = jnp.sum(spread, axis=2, keepdims=True)
        top = jnp.max(mass, axis=0, keepdims=True)
        share = jnp.exp(mass - top)
        result = jnp.sum(share * parts[:, h], axis=0) / jnp.sum(share, axis=0)
        for i in range(heads):
            at = (h * heads + i) * HEAD_WIDTH
            out_ref[:, at : at + HEAD_WIDTH] = result[i * rows : (i + 1) * rows].astype(BF16)

    @pl.when(own)
    def _():
        answers(servers - 1).wait_send()

    @pl.when(jnp.logical_not(own))
    def _():
        answers(servers).wait_send()


def on_device(
    n_ctx,
    n_head,
    queries,
    new_block_keys,
    new_block_values,
    stored_keys,
    stored_values,
    stretch_start,
    block_order,
):
    n = n_ctx * n_head
    rows = queries.shape[0]
    cache, width = stored_keys.shape
    crew = PAIR * n_head
    lines = QUERY_HEADS // n_head * rows
    total_keys = cache * PAIR + TILE * crew
    total_keys = (total_keys + 127) // 128 * 128
    dma = pltpu.SemaphoreType.DMA
    return pl.pallas_call(
        functools.partial(kernel, n_ctx, n_head),
        out_shape=jax.ShapeDtypeStruct(queries.shape, BF16),
        in_specs=[pl.BlockSpec(memory_space=pltpu.SMEM)]
        + [pl.BlockSpec(memory_space=pltpu.HBM)] * 6,
        out_specs=pl.BlockSpec(memory_space=pltpu.VMEM),
        scratch_shapes=[
            pltpu.SMEM(block_order.shape, jnp.int32),
            pltpu.VMEM((rows, queries.shape[1] + 2 * new_block_keys.shape[1]), BF16),
            pltpu.VMEM((n_head, lines, HEAD_WIDTH), BF16),
            pltpu.VMEM((n_head, lines, HEAD_WIDTH), BF16),
            pltpu.VMEM((n // 2, lines, HEAD_WIDTH), BF16),
            pltpu.VMEM((2, total_keys, width), BF16),
            pltpu.VMEM((n_head, 2, TILE, width), BF16),
            pltpu.VMEM((crew, 2, TILE, width), BF16),
            pltpu.VMEM((n // 2, lines + STAT_ROWS, HEAD_WIDTH), BF16),
            pltpu.VMEM((n // 2, lines + STAT_ROWS, HEAD_WIDTH), BF16),
            dma((3,)),
            dma((2,)),
            dma((3,)),
            dma((2,)),
            dma((2,)),
            dma((2,)),
        ],
        compiler_params=pltpu.CompilerParams(
            collective_id=0, has_side_effects=True, vmem_limit_bytes=48 * 1024 * 1024
        ),
    )(
        stretch_start,
        *[
            pltpu.with_memory_space_constraint(x, pltpu.HBM)
            for x in (
                block_order,
                queries,
                new_block_keys,
                new_block_values,
                stored_keys,
                stored_values,
            )
        ],
    )


def solution(mesh):
    return jax.shard_map(
        functools.partial(on_device, mesh.shape["ctx"], mesh.shape["head"]),
        mesh=mesh,
        in_specs=(
            P(("ctx", "head"), None),
            P(("ctx", "head"), None),
            P(("ctx", "head"), None),
            P("ctx", "head"),
            P("ctx", "head"),
            P(),
            P(),
        ),
        out_specs=P(("ctx", "head"), None),
        check_vma=False,
    )
```

```python
import functools
import math

import jax
import jax.numpy as jnp
from jax import lax
from jax.experimental import pallas as pl
from jax.experimental.pallas import tpu as pltpu
from jax.sharding import PartitionSpec as P

QUERY_HEADS = 16
HEAD_WIDTH = 128
NEG_FILL = -1e30
FAR = 2**30
TILE = 16
PAIR = 2
STAT_ROWS = 2
SCALE = 1.0 / math.sqrt(HEAD_WIDTH)
SCALE2 = SCALE * math.log2(math.e)
MESH = pl.DeviceIdType.MESH
F32 = jnp.float32
BF16 = jnp.bfloat16


def each(first, count, body):
    if count - first <= 64:
        for step in range(first, count):
            body(step)
    else:
        lax.fori_loop(first, count, lambda step, _: body(step), None)


def chunk_of(count):
    return max(c for c in range(1, 33) if count % c == 0)


def kernel(
    n_ctx,
    n_head,
    stretch_ref,
    order_hbm,
    q_hbm,
    nk_hbm,
    nv_hbm,
    k_hbm,
    v_hbm,
    out_ref,
    order_ref,
    stage,
    qsend,
    carry,
    qrecv,
    kv,
    kt,
    fresh,
    newbuf,
    osend,
    orecv,
    local_sem,
    q_send,
    q_recv,
    kv_send,
    kv_recv,
    o_sems,
):
    n = n_ctx * n_head
    rows = q_hbm.shape[0]
    cache, width = k_hbm.shape
    kv_heads = width // HEAD_WIDTH
    heads = QUERY_HEADS // n_head
    lines = heads * rows
    kv_lines = lines // kv_heads
    half = rows * n_head // 2
    per_half = half // rows
    crew = PAIR * n_head
    servers = n // 2
    plane = n_ctx // 4
    early = plane * n_head
    old_keys = cache * PAIR
    total_keys = kv.shape[1]
    ctx = lax.axis_index("ctx")
    head = lax.axis_index("head")
    me = ctx * n_head + head
    core = lax.rem(ctx, PAIR)
    lead = ctx - core
    seat = core * n_head + head
    desk = (ctx // PAIR) * n_head + head
    spot = lax.rem(me, servers)
    is_odd = core == 1
    is_low = ctx < 2 * plane
    is_early = ctx < plane
    is_relay = jnp.logical_not(is_early) & is_low
    own = jnp.where(is_low, core, 1 - core) == 1
    first_client = jnp.where(is_odd, 0, servers)

    def place(slot):
        return (slot // n_head, lax.rem(slot, n_head))

    def server_at(index):
        pair, h = place(index)
        return (pair * PAIR + jnp.where(is_low, 1, 0), h)

    def remote(source, target, send, recv, to):
        return pltpu.make_async_remote_copy(
            src_ref=source,
            dst_ref=target,
            send_sem=send,
            recv_sem=recv,
            device_id=to,
            device_id_type=MESH,
        )

    barrier = pltpu.get_barrier_semaphore()

    def signal(to):
        pl.semaphore_signal(barrier, inc=1, device_id=to, device_id_type=MESH)

    def greet(slot):
        @pl.when(slot != me)
        def _():
            signal(place(slot))

    @pl.when(is_odd)
    def _():
        each(0, early, lambda i: greet(early + lax.rem(me + i, early)))

    @pl.when(jnp.logical_not(is_odd))
    def _():
        each(0, servers, lambda i: greet(servers + lax.rem(me + i, servers)))

    @pl.when(is_relay)
    def _():
        signal((ctx - plane, head))

    for step in range(1, crew):
        c, h = place(lax.rem(seat + step, crew))
        signal((lead + c, h))

    own_rows = pl.ds(pl.multiple_of(core * cache, TILE), cache)
    q_width = q_hbm.shape[1]
    new_width = nk_hbm.shape[1]
    at = 0
    for source in (q_hbm, nk_hbm, nv_hbm):
        wide = source.shape[1]
        pltpu.make_async_copy(source, stage.at[:, at : at + wide], local_sem.at[0]).start()
        at += wide
    order_load = pltpu.make_async_copy(order_hbm, order_ref, local_sem.at[1])
    order_load.start()
    for t, source in enumerate((k_hbm, v_hbm)):
        pltpu.make_async_copy(source, kv.at[t, own_rows], local_sem.at[2]).start()

    pltpu.make_async_copy(stage, stage, local_sem.at[0]).wait()
    block = stage[:, :q_width].astype(F32)
    for h in range(n_head):
        pieces = [
            block[:, (h * heads + i) * HEAD_WIDTH : (h * heads + i + 1) * HEAD_WIDTH]
            for i in range(heads)
        ]
        qsend[h] = jnp.concatenate(pieces, axis=0).astype(BF16)
    blank = jnp.zeros((TILE - rows, width), F32)
    for t in range(2):
        new = stage[:, q_width + t * new_width : q_width + (t + 1) * new_width].astype(F32)
        for h in range(n_head):
            part = new[:, h * width : (h + 1) * width]
            fresh[h, t] = jnp.concatenate([part, blank], axis=0).astype(BF16)

    @pl.when(is_early)
    def _():
        pl.semaphore_wait(barrier, crew)

    @pl.when(jnp.logical_not(is_early) & own)
    def _():
        pl.semaphore_wait(barrier, servers - 1 + crew - 1)

    @pl.when(jnp.logical_not(is_early | own))
    def _():
        pl.semaphore_wait(barrier, servers + crew - 1)

    for t, source in enumerate((k_hbm, v_hbm)):
        remote(
            source, kv.at[t, own_rows], kv_send.at[0], kv_recv.at[0], (lead + 1 - core, head)
        ).start()
    for step in range(1, crew):
        to_core, to_head = place(lax.rem(seat + step, crew))
        remote(
            fresh.at[to_head],
            newbuf.at[seat],
            kv_send.at[1],
            kv_recv.at[1],
            (lead + to_core, to_head),
        ).start()

    wave = jnp.where(spot >= early, 1, 0)

    @pl.when(is_early)
    def _():
        remote(qsend, carry, q_send.at[0], q_recv.at[2], (ctx + plane, head)).start()

    @pl.when(is_relay)
    def _():
        remote(qsend, carry, q_send.at[0], q_recv.at[2], (ctx, head)).wait_recv()
        origin = me - early
        origin_desk = desk - early // PAIR

        def pass_on(step):
            to = servers - 1 - step

            @pl.when(jnp.logical_not(is_odd & ((to == origin_desk) | (to == desk))))
            def _():
                to_ctx, to_head = server_at(to)
                remote(
                    carry.at[to_head],
                    qrecv.at[origin],
                    q_send.at[1],
                    q_recv.at[0],
                    (to_ctx, to_head),
                ).start()

        each(0, servers, pass_on)

        @pl.when(is_odd)
        def _():
            qrecv[origin] = carry[head]

    def send_queries(step):
        to = lax.rem(desk + servers - step, servers)

        @pl.when(jnp.logical_not(own & (to == desk)))
        def _():
            to_ctx, to_head = server_at(to)
            remote(
                qsend.at[to_head],
                qrecv.at[spot],
                q_send.at[0],
                q_recv.at[wave],
                (to_ctx, to_head),
            ).start()

    @pl.when(jnp.logical_not(is_early))
    def _():
        each(1, servers + 1, send_queries)

    @pl.when(own)
    def _():
        qrecv[spot] = qsend[head]

    newbuf[seat] = fresh[head]
    spare = total_keys - old_keys - TILE * crew
    if spare:
        for t in range(2):
            kv[t, total_keys - spare :] = jnp.zeros((spare, width), BF16)

    order_load.wait()
    loaded = kv.at[:, own_rows]
    pltpu.make_async_copy(loaded, loaded, local_sem.at[2]).wait()

    def start_of(slot):
        return order_ref[slot // per_half] * half + lax.rem(slot, per_half) * rows

    split = (old_keys // 128) * 128
    column = lax.broadcasted_iota(jnp.int32, (1, total_keys), 1)
    cached = (column < old_keys) & (column + lead * cache < stretch_ref[0])
    key_pos = jnp.where(cached, -1, FAR)
    for j in range(crew):
        offset = column - (old_keys + TILE * j)
        pos = start_of(lead * n_head + j) + offset
        key_pos = jnp.where((offset >= 0) & (offset < rows), pos, key_pos)

    here = (ctx, head)
    remote(loaded, loaded, kv_send.at[0], kv_recv.at[0], here).wait()
    others = newbuf.at[pl.ds(0, crew - 1)]
    remote(others, others, kv_send.at[1], kv_recv.at[1], here).wait()
    for t in range(2):
        for j in range(crew):
            kv[t, old_keys + TILE * j : old_keys + TILE * (j + 1)] = newbuf[j, t]

    kt[...] = kv[0].T

    def expect(index, less, count):
        def wait_for(slots):
            block = qrecv.at[pl.ds(0, slots)]
            remote(block, block, q_send.at[0], q_recv.at[index], here).wait_recv()

        @pl.when(less)
        def _():
            wait_for(count - 1)

        @pl.when(jnp.logical_not(less))
        def _():
            wait_for(count)

    def attend(first, group):
        size = group * kv_lines
        block = qrecv[pl.ds(first, group)].astype(F32)
        tail = total_keys - split
        query_pos = jnp.concatenate(
            [
                jnp.full((kv_lines, tail), start_of(first_client + first + i), jnp.int32)
                for i in range(group)
            ],
            axis=0,
        )
        query_pos = query_pos + lax.rem(
            lax.broadcasted_iota(jnp.int32, (size, tail), 0), rows
        )
        scores = jnp.concatenate(
            [
                lax.dot_general(
                    block[:, g * kv_lines : (g + 1) * kv_lines]
                    .reshape(size, HEAD_WIDTH)
                    .astype(BF16),
                    kt[g * HEAD_WIDTH : (g + 1) * HEAD_WIDTH],
                    (((1,), (0,)), ((), ())),
                    preferred_element_type=F32,
                )
                for g in range(kv_heads)
            ],
            axis=0,
        )
        query_pos = jnp.concatenate([query_pos] * kv_heads, axis=0)
        old = jnp.where(key_pos[:, :split] < 0, scores[:, :split], NEG_FILL)
        new = jnp.where(key_pos[:, split:] <= query_pos, scores[:, split:], NEG_FILL)
        scores = jnp.concatenate([old, new], axis=1)
        peak = jnp.max(scores, axis=1, keepdims=True)
        weights = jnp.exp2((scores - peak) * SCALE2)
        total = jnp.sum(weights, axis=1, keepdims=True)
        sums = lax.dot_general(
            weights.astype(BF16), kv[1], (((1,), (0,)), ((), ())), preferred_element_type=F32
        )
        part = jnp.concatenate(
            [
                sums[g * size : (g + 1) * size, g * HEAD_WIDTH : (g + 1) * HEAD_WIDTH]
                for g in range(kv_heads)
            ],
            axis=0,
        )
        part = part / total
        mass = peak * SCALE + jnp.log(total)
        high = mass.astype(BF16).astype(F32)
        rest = mass - high
        mid = rest.astype(BF16).astype(F32)
        low = rest - mid
        lane = lax.broadcasted_iota(jnp.int32, (kv_heads * size, HEAD_WIDTH), 1)
        row = lax.broadcasted_iota(jnp.int32, (kv_heads * size, HEAD_WIDTH), 0)
        line = lax.rem(row, kv_lines) + kv_lines * (row // size)
        stat = jnp.where(lane < lines, high, jnp.where(lane < 2 * lines, mid, low))
        stat = jnp.where((lane < 3 * lines) & (lax.rem(lane, lines) == line), stat, 0.0)
        stat = stat.reshape(kv_heads, group, kv_lines, HEAD_WIDTH)
        stat = jnp.sum(jnp.sum(stat, axis=2, keepdims=True), axis=0)
        parts = [
            part[g * size : (g + 1) * size].reshape(group, kv_lines, HEAD_WIDTH)
            for g in range(kv_heads)
        ]
        osend[pl.ds(first, group), 0:lines] = jnp.concatenate(parts, axis=1).astype(BF16)
        osend[pl.ds(first, group), lines : lines + STAT_ROWS] = jnp.broadcast_to(
            stat, (group, STAT_ROWS, HEAD_WIDTH)
        ).astype(BF16)

    def send_part(index):
        slot = first_client + index

        @pl.when(slot != me)
        def _():
            remote(
                osend.at[index], orecv.at[desk], o_sems.at[0], o_sems.at[1], place(slot)
            ).start()

    for index, first, last in ((0, 0, early), (1, early, servers)):
        less = own & (wave == index)
        if index == 0:
            less = less | (own & is_relay)
        count = last - first
        expect(index, less, count)
        group = chunk_of(count)
        each(0, count // group, lambda i: attend(first + i * group, group))
        each(first, last, send_part)

    @pl.when(own)
    def _():
        orecv[desk] = osend[spot]

    def sent(sem, blocks):
        block = qrecv.at[pl.ds(0, blocks)]
        remote(block, block, sem, q_recv.at[0], here).wait_send()

    @pl.when(is_early)
    def _():
        sent(q_send.at[0], n_head)

    @pl.when(jnp.logical_not(is_early) & own)
    def _():
        sent(q_send.at[0], servers - 1)

    @pl.when(jnp.logical_not(is_early | own))
    def _():
        sent(q_send.at[0], servers)

    @pl.when(is_relay & is_odd)
    def _():
        sent(q_send.at[1], servers - 2)

    @pl.when(is_relay & jnp.logical_not(is_odd))
    def _():
        sent(q_send.at[1], servers)

    def answers(count):
        block = orecv.at[pl.ds(0, count)]
        return remote(block, block, o_sems.at[0], o_sems.at[1], here)

    @pl.when(own)
    def _():
        answers(servers - 1).wait_recv()

    @pl.when(jnp.logical_not(own))
    def _():
        answers(servers).wait_recv()

    lane = lax.broadcasted_iota(jnp.int32, (lines, HEAD_WIDTH), 1)
    line = lax.broadcasted_iota(jnp.int32, (lines, HEAD_WIDTH), 0)
    diagonal = (lane < 3 * lines) & (lax.rem(lane, lines) == line)
    shape = (n_ctx // PAIR, n_head)
    parts = orecv[:, 0:lines].astype(F32).reshape(*shape, lines, HEAD_WIDTH)
    stats = orecv[:, lines : lines + STAT_ROWS].astype(F32)
    stats = stats.reshape(*shape, STAT_ROWS, HEAD_WIDTH)
    for h in range(n_head):
        spread = jnp.where(diagonal[None], stats[:, h, 0:1], 0.0)
        mass = jnp.sum(spread, axis=2, keepdims=True)
        top = jnp.max(mass, axis=0, keepdims=True)
        share = jnp.exp(mass - top)
        result = jnp.sum(share * parts[:, h], axis=0) / jnp.sum(share, axis=0)
        for i in range(heads):
            at = (h * heads + i) * HEAD_WIDTH
            out_ref[:, at : at + HEAD_WIDTH] = result[i * rows : (i + 1) * rows].astype(BF16)

    @pl.when(own)
    def _():
        answers(servers - 1).wait_send()

    @pl.when(jnp.logical_not(own))
    def _():
        answers(servers).wait_send()


def on_device(
    n_ctx,
    n_head,
    queries,
    new_block_keys,
    new_block_values,
    stored_keys,
    stored_values,
    stretch_start,
    block_order,
):
    n = n_ctx * n_head
    rows = queries.shape[0]
    cache, width = stored_keys.shape
    crew = PAIR * n_head
    lines = QUERY_HEADS // n_head * rows
    total_keys = cache * PAIR + TILE * crew
    total_keys = (total_keys + 127) // 128 * 128
    dma = pltpu.SemaphoreType.DMA
    return pl.pallas_call(
        functools.partial(kernel, n_ctx, n_head),
        out_shape=jax.ShapeDtypeStruct(queries.shape, BF16),
        in_specs=[pl.BlockSpec(memory_space=pltpu.SMEM)]
        + [pl.BlockSpec(memory_space=pltpu.HBM)] * 6,
        out_specs=pl.BlockSpec(memory_space=pltpu.VMEM),
        scratch_shapes=[
            pltpu.SMEM(block_order.shape, jnp.int32),
            pltpu.VMEM((rows, queries.shape[1] + 2 * new_block_keys.shape[1]), BF16),
            pltpu.VMEM((n_head, lines, HEAD_WIDTH), BF16),
            pltpu.VMEM((n_head, lines, HEAD_WIDTH), BF16),
            pltpu.VMEM((n // 2, lines, HEAD_WIDTH), BF16),
            pltpu.VMEM((2, total_keys, width), BF16),
            pltpu.VMEM((width, total_keys), BF16),
            pltpu.VMEM((n_head, 2, TILE, width), BF16),
            pltpu.VMEM((crew, 2, TILE, width), BF16),
            pltpu.VMEM((n // 2, lines + STAT_ROWS, HEAD_WIDTH), BF16),
            pltpu.VMEM((n // 2, lines + STAT_ROWS, HEAD_WIDTH), BF16),
            dma((3,)),
            dma((2,)),
            dma((3,)),
            dma((2,)),
            dma((2,)),
            dma((2,)),
        ],
        compiler_params=pltpu.CompilerParams(
            collective_id=0, has_side_effects=True, vmem_limit_bytes=48 * 1024 * 1024
        ),
    )(
        stretch_start,
        *[
            pltpu.with_memory_space_constraint(x, pltpu.HBM)
            for x in (
                block_order,
                queries,
                new_block_keys,
                new_block_values,
                stored_keys,
                stored_values,
            )
        ],
    )


def solution(mesh):
    return jax.shard_map(
        functools.partial(on_device, mesh.shape["ctx"], mesh.shape["head"]),
        mesh=mesh,
        in_specs=(
            P(("ctx", "head"), None),
            P(("ctx", "head"), None),
            P(("ctx", "head"), None),
            P("ctx", "head"),
            P("ctx", "head"),
            P(),
            P(),
        ),
        out_specs=P(("ctx", "head"), None),
        check_vma=False,
    )
```

```python
import functools
import math

import jax
import jax.numpy as jnp
from jax import lax
from jax.experimental import pallas as pl
from jax.experimental.pallas import tpu as pltpu
from jax.sharding import PartitionSpec as P

QUERY_HEADS = 16
HEAD_WIDTH = 128
NEG_FILL = -1e30
FAR = 2**30
TILE = 16
PAIR = 2
STAT_ROWS = 2
SCALE = 1.0 / math.sqrt(HEAD_WIDTH)
SCALE2 = SCALE * math.log2(math.e)
MESH = pl.DeviceIdType.MESH
F32 = jnp.float32
BF16 = jnp.bfloat16


def each(first, count, body):
    if count - first <= 64:
        for step in range(first, count):
            body(step)
    else:
        lax.fori_loop(first, count, lambda step, _: body(step), None)


def chunk_of(count):
    return max(c for c in range(1, 33) if count % c == 0)


def kernel(
    n_ctx,
    n_head,
    stretch_ref,
    order_hbm,
    q_hbm,
    nk_hbm,
    nv_hbm,
    k_hbm,
    v_hbm,
    out_ref,
    order_ref,
    stage,
    qsend,
    carry,
    qrecv,
    kv,
    kt,
    fresh,
    osend,
    orecv,
    local_sem,
    q_sems,
    kv_sems,
    o_sems,
):
    n = n_ctx * n_head
    rows = q_hbm.shape[0]
    cache, width = k_hbm.shape
    kv_heads = width // HEAD_WIDTH
    heads = QUERY_HEADS // n_head
    lines = heads * rows
    kv_lines = lines // kv_heads
    half = rows * n_head // 2
    per_half = half // rows
    crew = PAIR * n_head
    servers = n // 2
    plane = n_ctx // 4
    early = plane * n_head
    old_keys = cache * PAIR
    total_keys = kv.shape[1]
    ctx = lax.axis_index("ctx")
    head = lax.axis_index("head")
    me = ctx * n_head + head
    core = lax.rem(ctx, PAIR)
    lead = ctx - core
    seat = core * n_head + head
    desk = (ctx // PAIR) * n_head + head
    spot = lax.rem(me, servers)
    is_odd = core == 1
    is_low = ctx < 2 * plane
    is_early = ctx < plane
    is_relay = jnp.logical_not(is_early) & is_low
    origin_ctx = ctx - plane + 1 - 2 * core
    own = jnp.where(is_low, core, 1 - core) == 1
    first_client = jnp.where(is_odd, 0, servers)

    def place(slot):
        return (slot // n_head, lax.rem(slot, n_head))

    def server_at(index):
        pair, h = place(index)
        return (pair * PAIR + jnp.where(is_low, 1, 0), h)

    def remote(source, target, send, recv, to):
        return pltpu.make_async_remote_copy(
            src_ref=source,
            dst_ref=target,
            send_sem=send,
            recv_sem=recv,
            device_id=to,
            device_id_type=MESH,
        )

    barrier = pltpu.get_barrier_semaphore()

    def signal(to):
        pl.semaphore_signal(barrier, inc=1, device_id=to, device_id_type=MESH)

    def greet(slot):
        @pl.when(slot != me)
        def _():
            signal(place(slot))

    @pl.when(is_odd)
    def _():
        each(0, early, lambda i: greet(early + lax.rem(me + i, early)))

    @pl.when(jnp.logical_not(is_odd))
    def _():
        each(0, servers, lambda i: greet(servers + lax.rem(me + i, servers)))

    @pl.when(is_relay)
    def _():
        signal((origin_ctx, head))

    for step in range(1, crew):
        c, h = place(lax.rem(seat + step, crew))
        signal((lead + c, h))

    own_rows = pl.ds(pl.multiple_of(core * cache, TILE), cache)
    q_width = q_hbm.shape[1]
    new_width = nk_hbm.shape[1]
    at = 0
    for source in (q_hbm, nk_hbm, nv_hbm):
        wide = source.shape[1]
        pltpu.make_async_copy(source, stage.at[:, at : at + wide], local_sem.at[0]).start()
        at += wide
    order_load = pltpu.make_async_copy(order_hbm, order_ref, local_sem.at[1])
    order_load.start()
    for t, source in enumerate((k_hbm, v_hbm)):
        pltpu.make_async_copy(source, kv.at[t, own_rows], local_sem.at[2]).start()

    pltpu.make_async_copy(stage, stage, local_sem.at[0]).wait()
    block = stage[:, :q_width].astype(F32)
    for h in range(n_head):
        pieces = [
            block[:, (h * heads + i) * HEAD_WIDTH : (h * heads + i + 1) * HEAD_WIDTH]
            for i in range(heads)
        ]
        qsend[h] = jnp.concatenate(pieces, axis=0).astype(BF16)
    blank = jnp.zeros((TILE - rows, width), F32)
    for t in range(2):
        new = stage[:, q_width + t * new_width : q_width + (t + 1) * new_width].astype(F32)
        for h in range(n_head):
            part = new[:, h * width : (h + 1) * width]
            fresh[h, t] = jnp.concatenate([part, blank], axis=0).astype(BF16)

    @pl.when(is_early)
    def _():
        pl.semaphore_wait(barrier, crew)

    @pl.when(jnp.logical_not(is_early) & own)
    def _():
        pl.semaphore_wait(barrier, servers - 1 + crew - 1)

    @pl.when(jnp.logical_not(is_early | own))
    def _():
        pl.semaphore_wait(barrier, servers + crew - 1)

    wave = jnp.where(spot >= early, 1, 0)

    @pl.when(is_early)
    def _():
        remote(qsend, carry, q_sems.at[3], q_sems.at[2], (ctx + plane + 1 - 2 * core, head)).start()

    @pl.when(is_relay)
    def _():
        remote(qsend, carry, q_sems.at[3], q_sems.at[2], (ctx, head)).wait_recv()

        def pass_on(step):
            to = servers - 1 - step
            stays = (to == desk) & is_odd
            returns = (to == origin_ctx // PAIR * n_head + head) & (
                lax.rem(origin_ctx, PAIR) == 1
            )

            @pl.when(jnp.logical_not(stays | returns))
            def _():
                to_ctx, to_head = server_at(to)
                remote(
                    carry.at[to_head],
                    qrecv.at[origin_ctx * n_head + head],
                    q_sems.at[3],
                    q_sems.at[0],
                    (to_ctx, to_head),
                ).start()

        each(0, servers, pass_on)

        @pl.when(is_odd)
        def _():
            qrecv[origin_ctx * n_head + head] = carry[head]

    def new_rows(seat):
        return pl.ds(pl.multiple_of(old_keys + TILE * seat, TILE), TILE)

    for t, source in enumerate((k_hbm, v_hbm)):
        remote(
            source, kv.at[t, own_rows], kv_sems.at[0], kv_sems.at[1], (lead + 1 - core, head)
        ).start()
    for step in range(1, crew):
        to_core, to_head = place(lax.rem(seat + step, crew))
        remote(
            fresh.at[to_head],
            kv.at[:, new_rows(seat)],
            kv_sems.at[0],
            kv_sems.at[1],
            (lead + to_core, to_head),
        ).start()

    def send_queries(step):
        to = lax.rem(desk + servers - step, servers)

        @pl.when(jnp.logical_not(own & (to == desk)))
        def _():
            to_ctx, to_head = server_at(to)
            remote(
                qsend.at[to_head],
                qrecv.at[spot],
                q_sems.at[3],
                q_sems.at[wave],
                (to_ctx, to_head),
            ).start()

    @pl.when(jnp.logical_not(is_early))
    def _():
        each(1, servers + 1, send_queries)

    @pl.when(own)
    def _():
        qrecv[spot] = qsend[head]

    kv[:, new_rows(seat)] = fresh[head]
    spare = total_keys - old_keys - TILE * crew
    if spare:
        for t in range(2):
            kv[t, total_keys - spare :] = jnp.zeros((spare, width), BF16)

    order_load.wait()
    loaded = kv.at[:, own_rows]
    pltpu.make_async_copy(loaded, loaded, local_sem.at[2]).wait()

    def start_of(slot):
        return order_ref[slot // per_half] * half + lax.rem(slot, per_half) * rows

    split = (old_keys // 128) * 128
    column = lax.broadcasted_iota(jnp.int32, (1, total_keys), 1)
    cached = (column < old_keys) & (column + lead * cache < stretch_ref[0])
    key_pos = jnp.where(cached, -1, FAR)
    for j in range(crew):
        offset = column - (old_keys + TILE * j)
        pos = start_of(lead * n_head + j) + offset
        key_pos = jnp.where((offset >= 0) & (offset < rows), pos, key_pos)

    here = (ctx, head)
    bulk = kv.at[:, pl.ds(0, cache + TILE * (crew - 1))]
    remote(bulk, bulk, kv_sems.at[0], kv_sems.at[1], here).wait()
    kt[...] = kv[0].T

    def expect(index, less, count):
        def wait_for(slots):
            block = qrecv.at[pl.ds(0, slots)]
            remote(block, block, q_sems.at[3], q_sems.at[index], here).wait_recv()

        @pl.when(less)
        def _():
            wait_for(count - 1)

        @pl.when(jnp.logical_not(less))
        def _():
            wait_for(count)

    def attend(first, group):
        size = group * kv_lines
        block = qrecv[pl.ds(first, group)].astype(F32)
        tail = total_keys - split
        query_pos = jnp.concatenate(
            [
                jnp.full((kv_lines, tail), start_of(first_client + first + i), jnp.int32)
                for i in range(group)
            ],
            axis=0,
        )
        query_pos = query_pos + lax.rem(
            lax.broadcasted_iota(jnp.int32, (size, tail), 0), rows
        )
        scores = jnp.concatenate(
            [
                lax.dot_general(
                    block[:, g * kv_lines : (g + 1) * kv_lines]
                    .reshape(size, HEAD_WIDTH)
                    .astype(BF16),
                    kt[g * HEAD_WIDTH : (g + 1) * HEAD_WIDTH],
                    (((1,), (0,)), ((), ())),
                    preferred_element_type=F32,
                )
                for g in range(kv_heads)
            ],
            axis=0,
        )
        query_pos = jnp.concatenate([query_pos] * kv_heads, axis=0)
        old = jnp.where(key_pos[:, :split] < 0, scores[:, :split], NEG_FILL)
        new = jnp.where(key_pos[:, split:] <= query_pos, scores[:, split:], NEG_FILL)
        scores = jnp.concatenate([old, new], axis=1)
        peak = jnp.max(scores, axis=1, keepdims=True)
        weights = jnp.exp2((scores - peak) * SCALE2)
        total = jnp.sum(weights, axis=1, keepdims=True)
        sums = lax.dot_general(
            weights.astype(BF16), kv[1], (((1,), (0,)), ((), ())), preferred_element_type=F32
        )
        part = jnp.concatenate(
            [
                sums[g * size : (g + 1) * size, g * HEAD_WIDTH : (g + 1) * HEAD_WIDTH]
                for g in range(kv_heads)
            ],
            axis=0,
        )
        part = part / total
        mass = peak * SCALE + jnp.log(total)
        high = mass.astype(BF16).astype(F32)
        rest = mass - high
        mid = rest.astype(BF16).astype(F32)
        low = rest - mid
        lane = lax.broadcasted_iota(jnp.int32, (kv_heads * size, HEAD_WIDTH), 1)
        row = lax.broadcasted_iota(jnp.int32, (kv_heads * size, HEAD_WIDTH), 0)
        line = lax.rem(row, kv_lines) + kv_lines * (row // size)
        stat = jnp.where(lane < lines, high, jnp.where(lane < 2 * lines, mid, low))
        stat = jnp.where((lane < 3 * lines) & (lax.rem(lane, lines) == line), stat, 0.0)
        stat = stat.reshape(kv_heads, group, kv_lines, HEAD_WIDTH)
        stat = jnp.sum(jnp.sum(stat, axis=2, keepdims=True), axis=0)
        parts = [
            part[g * size : (g + 1) * size].reshape(group, kv_lines, HEAD_WIDTH)
            for g in range(kv_heads)
        ]
        osend[pl.ds(first, group), 0:lines] = jnp.concatenate(parts, axis=1).astype(BF16)
        osend[pl.ds(first, group), lines : lines + STAT_ROWS] = jnp.broadcast_to(
            stat, (group, STAT_ROWS, HEAD_WIDTH)
        ).astype(BF16)

    def send_part(index):
        slot = first_client + index

        @pl.when(slot != me)
        def _():
            remote(
                osend.at[index], orecv.at[desk], o_sems.at[0], o_sems.at[1], place(slot)
            ).start()

    for index, first, last in ((0, 0, early), (1, early, servers)):
        less = own & (wave == index)
        if index == 0:
            less = less | (own & is_relay)
        count = last - first
        expect(index, less, count)
        group = chunk_of(count)
        each(0, count // group, lambda i: attend(first + i * group, group))
        each(first, last, send_part)

    @pl.when(own)
    def _():
        orecv[desk] = osend[spot]

    def sent(sem, blocks):
        block = qrecv.at[pl.ds(0, blocks)]
        remote(block, block, sem, q_sems.at[0], here).wait_send()

    @pl.when(is_early)
    def _():
        sent(q_sems.at[3], n_head)

    @pl.when(is_relay & own)
    def _():
        sent(q_sems.at[3], servers - 1)
        sent(q_sems.at[3], servers - 1)

    @pl.when(is_relay & jnp.logical_not(own))
    def _():
        sent(q_sems.at[3], servers)
        sent(q_sems.at[3], servers - 1)

    @pl.when(jnp.logical_not(is_low) & own)
    def _():
        sent(q_sems.at[3], servers - 1)

    @pl.when(jnp.logical_not(is_low | own))
    def _():
        sent(q_sems.at[3], servers)

    def answers(count):
        block = orecv.at[pl.ds(0, count)]
        return remote(block, block, o_sems.at[0], o_sems.at[1], here)

    @pl.when(own)
    def _():
        answers(servers - 1).wait_recv()

    @pl.when(jnp.logical_not(own))
    def _():
        answers(servers).wait_recv()

    lane = lax.broadcasted_iota(jnp.int32, (lines, HEAD_WIDTH), 1)
    line = lax.broadcasted_iota(jnp.int32, (lines, HEAD_WIDTH), 0)
    diagonal = (lane < 3 * lines) & (lax.rem(lane, lines) == line)
    shape = (n_ctx // PAIR, n_head)
    parts = orecv[:, 0:lines].astype(F32).reshape(*shape, lines, HEAD_WIDTH)
    stats = orecv[:, lines : lines + STAT_ROWS].astype(F32)
    stats = stats.reshape(*shape, STAT_ROWS, HEAD_WIDTH)
    for h in range(n_head):
        spread = jnp.where(diagonal[None], stats[:, h, 0:1], 0.0)
        mass = jnp.sum(spread, axis=2, keepdims=True)
        top = jnp.max(mass, axis=0, keepdims=True)
        share = jnp.exp(mass - top)
        result = jnp.sum(share * parts[:, h], axis=0) / jnp.sum(share, axis=0)
        for i in range(heads):
            at = (h * heads + i) * HEAD_WIDTH
            out_ref[:, at : at + HEAD_WIDTH] = result[i * rows : (i + 1) * rows].astype(BF16)

    @pl.when(own)
    def _():
        answers(servers - 1).wait_send()

    @pl.when(jnp.logical_not(own))
    def _():
        answers(servers).wait_send()


def on_device(
    n_ctx,
    n_head,
    queries,
    new_block_keys,
    new_block_values,
    stored_keys,
    stored_values,
    stretch_start,
    block_order,
):
    n = n_ctx * n_head
    rows = queries.shape[0]
    cache, width = stored_keys.shape
    crew = PAIR * n_head
    lines = QUERY_HEADS // n_head * rows
    total_keys = cache * PAIR + TILE * crew
    total_keys = (total_keys + 127) // 128 * 128
    dma = pltpu.SemaphoreType.DMA
    return pl.pallas_call(
        functools.partial(kernel, n_ctx, n_head),
        out_shape=jax.ShapeDtypeStruct(queries.shape, BF16),
        in_specs=[pl.BlockSpec(memory_space=pltpu.SMEM)]
        + [pl.BlockSpec(memory_space=pltpu.HBM)] * 6,
        out_specs=pl.BlockSpec(memory_space=pltpu.VMEM),
        scratch_shapes=[
            pltpu.SMEM(block_order.shape, jnp.int32),
            pltpu.VMEM((rows, queries.shape[1] + 2 * new_block_keys.shape[1]), BF16),
            pltpu.VMEM((n_head, lines, HEAD_WIDTH), BF16),
            pltpu.VMEM((n_head, lines, HEAD_WIDTH), BF16),
            pltpu.VMEM((n // 2, lines, HEAD_WIDTH), BF16),
            pltpu.VMEM((2, total_keys, width), BF16),
            pltpu.VMEM((width, total_keys), BF16),
            pltpu.VMEM((n_head, 2, TILE, width), BF16),
            pltpu.VMEM((n // 2, lines + STAT_ROWS, HEAD_WIDTH), BF16),
            pltpu.VMEM((n // 2, lines + STAT_ROWS, HEAD_WIDTH), BF16),
            dma((3,)),
            dma((4,)),
            dma((2,)),
            dma((2,)),
        ],
        compiler_params=pltpu.CompilerParams(
            collective_id=0, has_side_effects=True, vmem_limit_bytes=48 * 1024 * 1024
        ),
    )(
        stretch_start,
        *[
            pltpu.with_memory_space_constraint(x, pltpu.HBM)
            for x in (
                block_order,
                queries,
                new_block_keys,
                new_block_values,
                stored_keys,
                stored_values,
            )
        ],
    )


def solution(mesh):
    return jax.shard_map(
        functools.partial(on_device, mesh.shape["ctx"], mesh.shape["head"]),
        mesh=mesh,
        in_specs=(
            P(("ctx", "head"), None),
            P(("ctx", "head"), None),
            P(("ctx", "head"), None),
            P("ctx", "head"),
            P("ctx", "head"),
            P(),
            P(),
        ),
        out_specs=P(("ctx", "head"), None),
        check_vma=False,
    )
```

```python
import functools
import math

import jax
import jax.numpy as jnp
from jax import lax
from jax.experimental import pallas as pl
from jax.experimental.pallas import tpu as pltpu
from jax.sharding import PartitionSpec as P

QUERY_HEADS = 16
HEAD_WIDTH = 128
NEG_FILL = -1e30
FAR = 2**30
TILE = 16
PAIR = 2
STAT_ROWS = 2
SCALE = 1.0 / math.sqrt(HEAD_WIDTH)
SCALE2 = SCALE * math.log2(math.e)
MESH = pl.DeviceIdType.MESH
F32 = jnp.float32
BF16 = jnp.bfloat16


def each(first, count, body):
    if count - first <= 64:
        for step in range(first, count):
            body(step)
    else:
        lax.fori_loop(first, count, lambda step, _: body(step), None)


def chunk_of(count):
    return max(c for c in range(1, 33) if count % c == 0)


def kernel(
    n_ctx,
    n_head,
    stretch_ref,
    order_hbm,
    q_hbm,
    nk_hbm,
    nv_hbm,
    k_hbm,
    v_hbm,
    out_ref,
    order_ref,
    stage,
    qsend,
    carry,
    qrecv,
    kv,
    kt,
    fresh,
    osend,
    orecv,
    local_sem,
    q_sems,
    kv_sems,
):
    n = n_ctx * n_head
    rows = q_hbm.shape[0]
    cache, width = k_hbm.shape
    kv_heads = width // HEAD_WIDTH
    heads = QUERY_HEADS // n_head
    lines = heads * rows
    kv_lines = lines // kv_heads
    half = rows * n_head // 2
    per_half = half // rows
    crew = PAIR * n_head
    servers = n // 2
    plane = n_ctx // 4
    early = plane * n_head
    old_keys = cache * PAIR
    total_keys = kv.shape[1]
    ctx = lax.axis_index("ctx")
    head = lax.axis_index("head")
    me = ctx * n_head + head
    core = lax.rem(ctx, PAIR)
    lead = ctx - core
    seat = core * n_head + head
    desk = (ctx // PAIR) * n_head + head
    spot = lax.rem(me, servers)
    is_odd = core == 1
    is_low = ctx < 2 * plane
    is_early = ctx < plane
    is_relay = jnp.logical_not(is_early) & is_low
    origin_ctx = ctx - plane + 1 - 2 * core
    own = jnp.where(is_low, core, 1 - core) == 1
    first_client = jnp.where(is_odd, 0, servers)

    def place(slot):
        return (slot // n_head, lax.rem(slot, n_head))

    def server_at(index):
        pair, h = place(index)
        return (pair * PAIR + jnp.where(is_low, 1, 0), h)

    def remote(source, target, send, recv, to):
        return pltpu.make_async_remote_copy(
            src_ref=source,
            dst_ref=target,
            send_sem=send,
            recv_sem=recv,
            device_id=to,
            device_id_type=MESH,
        )

    barrier = pltpu.get_barrier_semaphore()

    def signal(to):
        pl.semaphore_signal(barrier, inc=1, device_id=to, device_id_type=MESH)

    def greet(slot):
        @pl.when(slot != me)
        def _():
            signal(place(slot))

    @pl.when(is_odd)
    def _():
        each(0, early, lambda i: greet(early + lax.rem(me + i, early)))

    @pl.when(jnp.logical_not(is_odd))
    def _():
        each(0, servers, lambda i: greet(servers + lax.rem(me + i, servers)))

    @pl.when(is_relay)
    def _():
        signal((origin_ctx, head))

    for step in range(1, crew):
        c, h = place(lax.rem(seat + step, crew))
        signal((lead + c, h))

    own_rows = pl.ds(pl.multiple_of(core * cache, TILE), cache)
    q_width = q_hbm.shape[1]
    new_width = nk_hbm.shape[1]
    at = 0
    for source in (q_hbm, nk_hbm, nv_hbm):
        wide = source.shape[1]
        pltpu.make_async_copy(source, stage.at[:, at : at + wide], local_sem.at[0]).start()
        at += wide
    order_load = pltpu.make_async_copy(order_hbm, order_ref, local_sem.at[1])
    order_load.start()
    for t, source in enumerate((k_hbm, v_hbm)):
        pltpu.make_async_copy(source, kv.at[t, own_rows], kv_sems.at[1]).start()

    pltpu.make_async_copy(stage, stage, local_sem.at[0]).wait()
    block = stage[:, :q_width].astype(F32)
    for h in range(n_head):
        pieces = [
            block[:, (h * heads + i) * HEAD_WIDTH : (h * heads + i + 1) * HEAD_WIDTH]
            for i in range(heads)
        ]
        qsend[h] = jnp.concatenate(pieces, axis=0).astype(BF16)
    blank = jnp.zeros((TILE - rows, width), F32)
    for t in range(2):
        new = stage[:, q_width + t * new_width : q_width + (t + 1) * new_width].astype(F32)
        for h in range(n_head):
            part = new[:, h * width : (h + 1) * width]
            fresh[h, t] = jnp.concatenate([part, blank], axis=0).astype(BF16)

    @pl.when(is_early)
    def _():
        pl.semaphore_wait(barrier, crew)

    @pl.when(jnp.logical_not(is_early) & own)
    def _():
        pl.semaphore_wait(barrier, servers - 1 + crew - 1)

    @pl.when(jnp.logical_not(is_early | own))
    def _():
        pl.semaphore_wait(barrier, servers + crew - 1)

    wave = jnp.where(spot >= early, 1, 0)

    @pl.when(is_early)
    def _():
        remote(qsend, carry, q_sems.at[3], q_sems.at[2], (ctx + plane + 1 - 2 * core, head)).start()

    @pl.when(is_relay)
    def _():
        remote(qsend, carry, q_sems.at[3], q_sems.at[2], (ctx, head)).wait_recv()

        def pass_on(step):
            to = servers - 1 - step
            stays = (to == desk) & is_odd
            returns = (to == origin_ctx // PAIR * n_head + head) & (
                lax.rem(origin_ctx, PAIR) == 1
            )

            @pl.when(jnp.logical_not(stays | returns))
            def _():
                to_ctx, to_head = server_at(to)
                remote(
                    carry.at[to_head],
                    qrecv.at[origin_ctx * n_head + head],
                    q_sems.at[3],
                    q_sems.at[0],
                    (to_ctx, to_head),
                ).start()

        each(0, servers, pass_on)

        @pl.when(is_odd)
        def _():
            qrecv[origin_ctx * n_head + head] = carry[head]

    def new_rows(seat):
        return pl.ds(pl.multiple_of(old_keys + TILE * seat, TILE), TILE)

    for t, source in enumerate((k_hbm, v_hbm)):
        remote(
            source, kv.at[t, own_rows], q_sems.at[3], kv_sems.at[1], (lead + 1 - core, head)
        ).start()
    for step in range(1, crew):
        to_core, to_head = place(lax.rem(seat + step, crew))
        remote(
            fresh.at[to_head],
            kv.at[:, new_rows(seat)],
            q_sems.at[3],
            kv_sems.at[1],
            (lead + to_core, to_head),
        ).start()

    def send_queries(step):
        to = lax.rem(desk + servers - step, servers)

        @pl.when(jnp.logical_not(own & (to == desk)))
        def _():
            to_ctx, to_head = server_at(to)
            remote(
                qsend.at[to_head],
                qrecv.at[spot],
                q_sems.at[3],
                q_sems.at[wave],
                (to_ctx, to_head),
            ).start()

    @pl.when(jnp.logical_not(is_early))
    def _():
        each(1, servers + 1, send_queries)

    @pl.when(own)
    def _():
        qrecv[spot] = qsend[head]

    kv[:, new_rows(seat)] = fresh[head]
    spare = total_keys - old_keys - TILE * crew
    if spare:
        for t in range(2):
            kv[t, total_keys - spare :] = jnp.zeros((spare, width), BF16)

    order_load.wait()

    def start_of(slot):
        return order_ref[slot // per_half] * half + lax.rem(slot, per_half) * rows

    split = (old_keys // 128) * 128
    column = lax.broadcasted_iota(jnp.int32, (1, total_keys), 1)
    cached = (column < old_keys) & (column + lead * cache < stretch_ref[0])
    key_pos = jnp.where(cached, -1, FAR)
    for j in range(crew):
        offset = column - (old_keys + TILE * j)
        pos = start_of(lead * n_head + j) + offset
        key_pos = jnp.where((offset >= 0) & (offset < rows), pos, key_pos)

    here = (ctx, head)
    bulk = kv.at[:, pl.ds(0, 2 * cache + TILE * (crew - 1))]
    remote(bulk, bulk, q_sems.at[3], kv_sems.at[1], here).wait_recv()
    kt[...] = kv[0].T

    def expect(index, less, count):
        def wait_for(slots):
            block = qrecv.at[pl.ds(0, slots)]
            remote(block, block, q_sems.at[3], q_sems.at[index], here).wait_recv()

        @pl.when(less)
        def _():
            wait_for(count - 1)

        @pl.when(jnp.logical_not(less))
        def _():
            wait_for(count)

    def attend(first, group):
        size = group * kv_lines
        block = qrecv[pl.ds(first, group)].astype(F32)
        tail = total_keys - split
        query_pos = jnp.concatenate(
            [
                jnp.full((kv_lines, tail), start_of(first_client + first + i), jnp.int32)
                for i in range(group)
            ],
            axis=0,
        )
        query_pos = query_pos + lax.rem(
            lax.broadcasted_iota(jnp.int32, (size, tail), 0), rows
        )
        scores = jnp.concatenate(
            [
                lax.dot_general(
                    block[:, g * kv_lines : (g + 1) * kv_lines]
                    .reshape(size, HEAD_WIDTH)
                    .astype(BF16),
                    kt[g * HEAD_WIDTH : (g + 1) * HEAD_WIDTH],
                    (((1,), (0,)), ((), ())),
                    preferred_element_type=F32,
                )
                for g in range(kv_heads)
            ],
            axis=0,
        )
        query_pos = jnp.concatenate([query_pos] * kv_heads, axis=0)
        old = jnp.where(key_pos[:, :split] < 0, scores[:, :split], NEG_FILL)
        new = jnp.where(key_pos[:, split:] <= query_pos, scores[:, split:], NEG_FILL)
        scores = jnp.concatenate([old, new], axis=1)
        peak = jnp.max(scores, axis=1, keepdims=True)
        weights = jnp.exp2((scores - peak) * SCALE2)
        total = jnp.sum(weights, axis=1, keepdims=True)
        sums = lax.dot_general(
            weights.astype(BF16), kv[1], (((1,), (0,)), ((), ())), preferred_element_type=F32
        )
        part = jnp.concatenate(
            [
                sums[g * size : (g + 1) * size, g * HEAD_WIDTH : (g + 1) * HEAD_WIDTH]
                for g in range(kv_heads)
            ],
            axis=0,
        )
        part = part / total
        mass = peak * SCALE + jnp.log(total)
        high = mass.astype(BF16).astype(F32)
        rest = mass - high
        mid = rest.astype(BF16).astype(F32)
        low = rest - mid
        lane = lax.broadcasted_iota(jnp.int32, (kv_heads * size, HEAD_WIDTH), 1)
        row = lax.broadcasted_iota(jnp.int32, (kv_heads * size, HEAD_WIDTH), 0)
        line = lax.rem(row, kv_lines) + kv_lines * (row // size)
        stat = jnp.where(lane < lines, high, jnp.where(lane < 2 * lines, mid, low))
        stat = jnp.where((lane < 3 * lines) & (lax.rem(lane, lines) == line), stat, 0.0)
        stat = stat.reshape(kv_heads, group, kv_lines, HEAD_WIDTH)
        stat = jnp.sum(jnp.sum(stat, axis=2, keepdims=True), axis=0)
        parts = [
            part[g * size : (g + 1) * size].reshape(group, kv_lines, HEAD_WIDTH)
            for g in range(kv_heads)
        ]
        osend[pl.ds(first, group), 0:lines] = jnp.concatenate(parts, axis=1).astype(BF16)
        osend[pl.ds(first, group), lines : lines + STAT_ROWS] = jnp.broadcast_to(
            stat, (group, STAT_ROWS, HEAD_WIDTH)
        ).astype(BF16)

    def send_part(index):
        slot = first_client + index

        @pl.when(slot != me)
        def _():
            remote(
                osend.at[index], orecv.at[desk], q_sems.at[3], kv_sems.at[0], place(slot)
            ).start()

    for index, first, last in ((0, 0, early), (1, early, servers)):
        less = own & (wave == index)
        if index == 0:
            less = less | (own & is_relay)
        count = last - first
        expect(index, less, count)
        group = chunk_of(count)
        each(0, count // group, lambda i: attend(first + i * group, group))
        each(first, last, send_part)

    @pl.when(own)
    def _():
        orecv[desk] = osend[spot]

    def sent(sem, blocks):
        block = qrecv.at[pl.ds(0, blocks)]
        remote(block, block, sem, q_sems.at[0], here).wait_send()

    @pl.when(is_early)
    def _():
        sent(q_sems.at[3], n_head)

    @pl.when(is_relay & own)
    def _():
        sent(q_sems.at[3], servers - 1)
        sent(q_sems.at[3], servers - 1)

    @pl.when(is_relay & jnp.logical_not(own))
    def _():
        sent(q_sems.at[3], servers)
        sent(q_sems.at[3], servers - 1)

    @pl.when(jnp.logical_not(is_low) & own)
    def _():
        sent(q_sems.at[3], servers - 1)

    @pl.when(jnp.logical_not(is_low | own))
    def _():
        sent(q_sems.at[3], servers)

    def answers(count):
        block = orecv.at[pl.ds(0, count)]
        return remote(block, block, q_sems.at[3], kv_sems.at[0], here)

    @pl.when(own)
    def _():
        answers(servers - 1).wait_recv()

    @pl.when(jnp.logical_not(own))
    def _():
        answers(servers).wait_recv()

    lane = lax.broadcasted_iota(jnp.int32, (lines, HEAD_WIDTH), 1)
    line = lax.broadcasted_iota(jnp.int32, (lines, HEAD_WIDTH), 0)
    diagonal = (lane < 3 * lines) & (lax.rem(lane, lines) == line)
    shape = (n_ctx // PAIR, n_head)
    parts = orecv[:, 0:lines].astype(F32).reshape(*shape, lines, HEAD_WIDTH)
    stats = orecv[:, lines : lines + STAT_ROWS].astype(F32)
    stats = stats.reshape(*shape, STAT_ROWS, HEAD_WIDTH)
    for h in range(n_head):
        spread = jnp.where(diagonal[None], stats[:, h, 0:1], 0.0)
        mass = jnp.sum(spread, axis=2, keepdims=True)
        top = jnp.max(mass, axis=0, keepdims=True)
        share = jnp.exp(mass - top)
        result = jnp.sum(share * parts[:, h], axis=0) / jnp.sum(share, axis=0)
        for i in range(heads):
            at = (h * heads + i) * HEAD_WIDTH
            out_ref[:, at : at + HEAD_WIDTH] = result[i * rows : (i + 1) * rows].astype(BF16)

    shipped = kv.at[:, pl.ds(0, cache + TILE * (crew - 1))]
    remote(shipped, shipped, q_sems.at[3], kv_sems.at[1], here).wait_send()

    @pl.when(own)
    def _():
        answers(servers - 1).wait_send()

    @pl.when(jnp.logical_not(own))
    def _():
        answers(servers).wait_send()


def on_device(
    n_ctx,
    n_head,
    queries,
    new_block_keys,
    new_block_values,
    stored_keys,
    stored_values,
    stretch_start,
    block_order,
):
    n = n_ctx * n_head
    rows = queries.shape[0]
    cache, width = stored_keys.shape
    crew = PAIR * n_head
    lines = QUERY_HEADS // n_head * rows
    total_keys = cache * PAIR + TILE * crew
    total_keys = (total_keys + 127) // 128 * 128
    dma = pltpu.SemaphoreType.DMA
    return pl.pallas_call(
        functools.partial(kernel, n_ctx, n_head),
        out_shape=jax.ShapeDtypeStruct(queries.shape, BF16),
        in_specs=[pl.BlockSpec(memory_space=pltpu.SMEM)]
        + [pl.BlockSpec(memory_space=pltpu.HBM)] * 6,
        out_specs=pl.BlockSpec(memory_space=pltpu.VMEM),
        scratch_shapes=[
            pltpu.SMEM(block_order.shape, jnp.int32),
            pltpu.VMEM((rows, queries.shape[1] + 2 * new_block_keys.shape[1]), BF16),
            pltpu.VMEM((n_head, lines, HEAD_WIDTH), BF16),
            pltpu.VMEM((n_head, lines, HEAD_WIDTH), BF16),
            pltpu.VMEM((n // 2, lines, HEAD_WIDTH), BF16),
            pltpu.VMEM((2, total_keys, width), BF16),
            pltpu.VMEM((width, total_keys), BF16),
            pltpu.VMEM((n_head, 2, TILE, width), BF16),
            pltpu.VMEM((n // 2, lines + STAT_ROWS, HEAD_WIDTH), BF16),
            pltpu.VMEM((n // 2, lines + STAT_ROWS, HEAD_WIDTH), BF16),
            dma((2,)),
            dma((4,)),
            dma((2,)),
        ],
        compiler_params=pltpu.CompilerParams(
            collective_id=0, has_side_effects=True, vmem_limit_bytes=48 * 1024 * 1024
        ),
    )(
        stretch_start,
        *[
            pltpu.with_memory_space_constraint(x, pltpu.HBM)
            for x in (
                block_order,
                queries,
                new_block_keys,
                new_block_values,
                stored_keys,
                stored_values,
            )
        ],
    )


def solution(mesh):
    return jax.shard_map(
        functools.partial(on_device, mesh.shape["ctx"], mesh.shape["head"]),
        mesh=mesh,
        in_specs=(
            P(("ctx", "head"), None),
            P(("ctx", "head"), None),
            P(("ctx", "head"), None),
            P("ctx", "head"),
            P("ctx", "head"),
            P(),
            P(),
        ),
        out_specs=P(("ctx", "head"), None),
        check_vma=False,
    )
```

```python
import functools
import math

import jax
import jax.numpy as jnp
from jax import lax
from jax.experimental import pallas as pl
from jax.experimental.pallas import tpu as pltpu
from jax.sharding import PartitionSpec as P

QUERY_HEADS = 16
HEAD_WIDTH = 128
NEG_FILL = -1e30
FAR = 2**30
TILE = 16
PAIR = 2
STAT_ROWS = 2
SCALE = 1.0 / math.sqrt(HEAD_WIDTH)
SCALE2 = SCALE * math.log2(math.e)
MESH = pl.DeviceIdType.MESH
F32 = jnp.float32
BF16 = jnp.bfloat16


def each(first, count, body):
    if count - first <= 64:
        for step in range(first, count):
            body(step)
    else:
        lax.fori_loop(first, count, lambda step, _: body(step), None)


def chunk_of(count):
    return max(c for c in range(1, 33) if count % c == 0)


def kernel(
    n_ctx,
    n_head,
    stretch_ref,
    order_hbm,
    q_hbm,
    nk_hbm,
    nv_hbm,
    k_hbm,
    v_hbm,
    out_ref,
    order_ref,
    stage,
    qsend,
    carry,
    qrecv,
    kv,
    kt,
    fresh,
    osend,
    orecv,
    local_sem,
    q_sems,
    kv_sems,
):
    n = n_ctx * n_head
    rows = q_hbm.shape[0]
    cache, width = k_hbm.shape
    kv_heads = width // HEAD_WIDTH
    heads = QUERY_HEADS // n_head
    lines = heads * rows
    kv_lines = lines // kv_heads
    half = rows * n_head // 2
    per_half = half // rows
    crew = PAIR * n_head
    servers = n // 2
    plane = n_ctx // 4
    early = plane * n_head
    old_keys = cache * PAIR
    total_keys = kv.shape[1]
    ctx = lax.axis_index("ctx")
    head = lax.axis_index("head")
    me = ctx * n_head + head
    core = lax.rem(ctx, PAIR)
    lead = ctx - core
    seat = core * n_head + head
    desk = (ctx // PAIR) * n_head + head
    spot = lax.rem(me, servers)
    is_odd = core == 1
    is_low = ctx < 2 * plane
    is_early = ctx < plane
    is_relay = jnp.logical_not(is_early) & is_low
    origin_ctx = ctx - plane + 1 - 2 * core
    own = jnp.where(is_low, core, 1 - core) == 1
    first_client = jnp.where(is_odd, 0, servers)

    def place(slot):
        return (slot // n_head, lax.rem(slot, n_head))

    def server_at(index):
        pair, h = place(index)
        return (pair * PAIR + jnp.where(is_low, 1, 0), h)

    def remote(source, target, send, recv, to):
        return pltpu.make_async_remote_copy(
            src_ref=source,
            dst_ref=target,
            send_sem=send,
            recv_sem=recv,
            device_id=to,
            device_id_type=MESH,
        )

    barrier = pltpu.get_barrier_semaphore()

    def signal(to):
        pl.semaphore_signal(barrier, inc=1, device_id=to, device_id_type=MESH)

    def greet(slot):
        @pl.when(slot != me)
        def _():
            signal(place(slot))

    @pl.when(is_odd)
    def _():
        each(early, 2 * early, greet)

    @pl.when(jnp.logical_not(is_odd))
    def _():
        each(0, servers, lambda i: greet(servers + lax.rem(me + i, servers)))

    @pl.when(is_relay)
    def _():
        signal((origin_ctx, head))

    for step in range(1, crew):
        c, h = place(lax.rem(seat + step, crew))
        signal((lead + c, h))

    own_rows = pl.ds(pl.multiple_of(core * cache, TILE), cache)
    q_width = q_hbm.shape[1]
    new_width = nk_hbm.shape[1]
    at = 0
    for source in (q_hbm, nk_hbm, nv_hbm):
        wide = source.shape[1]
        pltpu.make_async_copy(source, stage.at[:, at : at + wide], local_sem.at[0]).start()
        at += wide
    order_load = pltpu.make_async_copy(order_hbm, order_ref, local_sem.at[1])
    order_load.start()
    for t, source in enumerate((k_hbm, v_hbm)):
        pltpu.make_async_copy(source, kv.at[t, own_rows], kv_sems.at[1]).start()

    pltpu.make_async_copy(stage, stage, local_sem.at[0]).wait()
    block = stage[:, :q_width].astype(F32)
    for h in range(n_head):
        pieces = [
            block[:, (h * heads + i) * HEAD_WIDTH : (h * heads + i + 1) * HEAD_WIDTH]
            for i in range(heads)
        ]
        qsend[h] = jnp.concatenate(pieces, axis=0).astype(BF16)
    blank = jnp.zeros((TILE - rows, width), F32)
    for t in range(2):
        new = stage[:, q_width + t * new_width : q_width + (t + 1) * new_width].astype(F32)
        for h in range(n_head):
            part = new[:, h * width : (h + 1) * width]
            fresh[h, t] = jnp.concatenate([part, blank], axis=0).astype(BF16)

    @pl.when(is_early)
    def _():
        pl.semaphore_wait(barrier, crew)

    @pl.when(jnp.logical_not(is_early) & own)
    def _():
        pl.semaphore_wait(barrier, servers - 1 + crew - 1)

    @pl.when(jnp.logical_not(is_early | own))
    def _():
        pl.semaphore_wait(barrier, servers + crew - 1)

    wave = jnp.where(spot >= early, 1, 0)

    @pl.when(is_early)
    def _():
        remote(qsend, carry, q_sems.at[3], q_sems.at[2], (ctx + plane + 1 - 2 * core, head)).start()

    @pl.when(is_relay)
    def _():
        remote(qsend, carry, q_sems.at[3], q_sems.at[2], (ctx, head)).wait_recv()

        origin_desk = origin_ctx // PAIR * n_head + head
        turn = 2 * servers - 1 - lax.rem(origin_desk, 4) * (servers // 4)

        def pass_on(step):
            to = lax.rem(turn - step, servers)
            stays = (to == desk) & is_odd
            returns = (to == origin_desk) & (
                lax.rem(origin_ctx, PAIR) == 1
            )

            @pl.when(jnp.logical_not(stays | returns))
            def _():
                to_ctx, to_head = server_at(to)
                remote(
                    carry.at[to_head],
                    qrecv.at[origin_ctx * n_head + head],
                    q_sems.at[3],
                    q_sems.at[0],
                    (to_ctx, to_head),
                ).start()

        each(0, servers, pass_on)

        @pl.when(is_odd)
        def _():
            qrecv[origin_ctx * n_head + head] = carry[head]

    def new_rows(seat):
        return pl.ds(pl.multiple_of(old_keys + TILE * seat, TILE), TILE)

    for t, source in enumerate((k_hbm, v_hbm)):
        remote(
            source, kv.at[t, own_rows], q_sems.at[3], kv_sems.at[1], (lead + 1 - core, head)
        ).start()
    for step in range(1, crew):
        to_core, to_head = place(lax.rem(seat + step, crew))
        remote(
            fresh.at[to_head],
            kv.at[:, new_rows(seat)],
            q_sems.at[3],
            kv_sems.at[1],
            (lead + to_core, to_head),
        ).start()

    def send_queries(step):
        to = lax.rem(desk + servers - step, servers)

        @pl.when(jnp.logical_not(own & (to == desk)))
        def _():
            to_ctx, to_head = server_at(to)
            remote(
                qsend.at[to_head],
                qrecv.at[spot],
                q_sems.at[3],
                q_sems.at[wave],
                (to_ctx, to_head),
            ).start()

    @pl.when(jnp.logical_not(is_early))
    def _():
        each(1, servers + 1, send_queries)

    @pl.when(own)
    def _():
        qrecv[spot] = qsend[head]

    kv[:, new_rows(seat)] = fresh[head]
    spare = total_keys - old_keys - TILE * crew
    if spare:
        for t in range(2):
            kv[t, total_keys - spare :] = jnp.zeros((spare, width), BF16)

    order_load.wait()

    def start_of(slot):
        return order_ref[slot // per_half] * half + lax.rem(slot, per_half) * rows

    split = (old_keys // 128) * 128
    column = lax.broadcasted_iota(jnp.int32, (1, total_keys), 1)
    cached = (column < old_keys) & (column + lead * cache < stretch_ref[0])
    key_pos = jnp.where(cached, -1, FAR)
    for j in range(crew):
        offset = column - (old_keys + TILE * j)
        pos = start_of(lead * n_head + j) + offset
        key_pos = jnp.where((offset >= 0) & (offset < rows), pos, key_pos)

    here = (ctx, head)
    bulk = kv.at[:, pl.ds(0, 2 * cache + TILE * (crew - 1))]
    remote(bulk, bulk, q_sems.at[3], kv_sems.at[1], here).wait_recv()
    kt[...] = kv[0].T

    def expect(index, less, count):
        def wait_for(slots):
            block = qrecv.at[pl.ds(0, slots)]
            remote(block, block, q_sems.at[3], q_sems.at[index], here).wait_recv()

        @pl.when(less)
        def _():
            wait_for(count - 1)

        @pl.when(jnp.logical_not(less))
        def _():
            wait_for(count)

    def attend(first, group):
        size = group * kv_lines
        block = qrecv[pl.ds(first, group)].astype(F32)
        tail = total_keys - split
        query_pos = jnp.concatenate(
            [
                jnp.full((kv_lines, tail), start_of(first_client + first + i), jnp.int32)
                for i in range(group)
            ],
            axis=0,
        )
        query_pos = query_pos + lax.rem(
            lax.broadcasted_iota(jnp.int32, (size, tail), 0), rows
        )
        scores = jnp.concatenate(
            [
                lax.dot_general(
                    block[:, g * kv_lines : (g + 1) * kv_lines]
                    .reshape(size, HEAD_WIDTH)
                    .astype(BF16),
                    kt[g * HEAD_WIDTH : (g + 1) * HEAD_WIDTH],
                    (((1,), (0,)), ((), ())),
                    preferred_element_type=F32,
                )
                for g in range(kv_heads)
            ],
            axis=0,
        )
        query_pos = jnp.concatenate([query_pos] * kv_heads, axis=0)
        old = jnp.where(key_pos[:, :split] < 0, scores[:, :split], NEG_FILL)
        new = jnp.where(key_pos[:, split:] <= query_pos, scores[:, split:], NEG_FILL)
        scores = jnp.concatenate([old, new], axis=1)
        peak = jnp.max(scores, axis=1, keepdims=True)
        weights = jnp.exp2((scores - peak) * SCALE2)
        total = jnp.sum(weights, axis=1, keepdims=True)
        sums = lax.dot_general(
            weights.astype(BF16), kv[1], (((1,), (0,)), ((), ())), preferred_element_type=F32
        )
        part = jnp.concatenate(
            [
                sums[g * size : (g + 1) * size, g * HEAD_WIDTH : (g + 1) * HEAD_WIDTH]
                for g in range(kv_heads)
            ],
            axis=0,
        )
        part = part / total
        mass = peak * SCALE + jnp.log(total)
        high = mass.astype(BF16).astype(F32)
        rest = mass - high
        mid = rest.astype(BF16).astype(F32)
        low = rest - mid
        lane = lax.broadcasted_iota(jnp.int32, (kv_heads * size, HEAD_WIDTH), 1)
        row = lax.broadcasted_iota(jnp.int32, (kv_heads * size, HEAD_WIDTH), 0)
        line = lax.rem(row, kv_lines) + kv_lines * (row // size)
        stat = jnp.where(lane < lines, high, jnp.where(lane < 2 * lines, mid, low))
        stat = jnp.where((lane < 3 * lines) & (lax.rem(lane, lines) == line), stat, 0.0)
        stat = stat.reshape(kv_heads, group, kv_lines, HEAD_WIDTH)
        stat = jnp.sum(jnp.sum(stat, axis=2, keepdims=True), axis=0)
        parts = [
            part[g * size : (g + 1) * size].reshape(group, kv_lines, HEAD_WIDTH)
            for g in range(kv_heads)
        ]
        osend[pl.ds(first, group), 0:lines] = jnp.concatenate(parts, axis=1).astype(BF16)
        osend[pl.ds(first, group), lines : lines + STAT_ROWS] = jnp.broadcast_to(
            stat, (group, STAT_ROWS, HEAD_WIDTH)
        ).astype(BF16)

    def send_part(index):
        slot = first_client + index

        @pl.when(slot != me)
        def _():
            remote(
                osend.at[index], orecv.at[desk], q_sems.at[3], kv_sems.at[0], place(slot)
            ).start()

    for index, first, last in ((0, 0, early), (1, early, servers)):
        less = own & (wave == index)
        if index == 0:
            less = less | (own & is_relay)
        count = last - first
        expect(index, less, count)
        group = chunk_of(count)
        each(0, count // group, lambda i: attend(first + i * group, group))
        each(first, last, send_part)

    @pl.when(own)
    def _():
        orecv[desk] = osend[spot]

    def sent(sem, blocks):
        block = qrecv.at[pl.ds(0, blocks)]
        remote(block, block, sem, q_sems.at[0], here).wait_send()

    @pl.when(is_early)
    def _():
        sent(q_sems.at[3], n_head)

    @pl.when(is_relay & own)
    def _():
        sent(q_sems.at[3], servers - 1)
        sent(q_sems.at[3], servers - 1)

    @pl.when(is_relay & jnp.logical_not(own))
    def _():
        sent(q_sems.at[3], servers)
        sent(q_sems.at[3], servers - 1)

    @pl.when(jnp.logical_not(is_low) & own)
    def _():
        sent(q_sems.at[3], servers - 1)

    @pl.when(jnp.logical_not(is_low | own))
    def _():
        sent(q_sems.at[3], servers)

    def answers(count):
        block = orecv.at[pl.ds(0, count)]
        return remote(block, block, q_sems.at[3], kv_sems.at[0], here)

    @pl.when(own)
    def _():
        answers(servers - 1).wait_recv()

    @pl.when(jnp.logical_not(own))
    def _():
        answers(servers).wait_recv()

    lane = lax.broadcasted_iota(jnp.int32, (lines, HEAD_WIDTH), 1)
    line = lax.broadcasted_iota(jnp.int32, (lines, HEAD_WIDTH), 0)
    diagonal = (lane < 3 * lines) & (lax.rem(lane, lines) == line)
    shape = (n_ctx // PAIR, n_head)
    parts = orecv[:, 0:lines].astype(F32).reshape(*shape, lines, HEAD_WIDTH)
    stats = orecv[:, lines : lines + STAT_ROWS].astype(F32)
    stats = stats.reshape(*shape, STAT_ROWS, HEAD_WIDTH)
    for h in range(n_head):
        spread = jnp.where(diagonal[None], stats[:, h, 0:1], 0.0)
        mass = jnp.sum(spread, axis=2, keepdims=True)
        top = jnp.max(mass, axis=0, keepdims=True)
        share = jnp.exp(mass - top)
        result = jnp.sum(share * parts[:, h], axis=0) / jnp.sum(share, axis=0)
        for i in range(heads):
            at = (h * heads + i) * HEAD_WIDTH
            out_ref[:, at : at + HEAD_WIDTH] = result[i * rows : (i + 1) * rows].astype(BF16)

    shipped = kv.at[:, pl.ds(0, cache + TILE * (crew - 1))]
    remote(shipped, shipped, q_sems.at[3], kv_sems.at[1], here).wait_send()

    @pl.when(own)
    def _():
        answers(servers - 1).wait_send()

    @pl.when(jnp.logical_not(own))
    def _():
        answers(servers).wait_send()


def on_device(
    n_ctx,
    n_head,
    queries,
    new_block_keys,
    new_block_values,
    stored_keys,
    stored_values,
    stretch_start,
    block_order,
):
    n = n_ctx * n_head
    rows = queries.shape[0]
    cache, width = stored_keys.shape
    crew = PAIR * n_head
    lines = QUERY_HEADS // n_head * rows
    total_keys = cache * PAIR + TILE * crew
    total_keys = (total_keys + 127) // 128 * 128
    dma = pltpu.SemaphoreType.DMA
    return pl.pallas_call(
        functools.partial(kernel, n_ctx, n_head),
        out_shape=jax.ShapeDtypeStruct(queries.shape, BF16),
        in_specs=[pl.BlockSpec(memory_space=pltpu.SMEM)]
        + [pl.BlockSpec(memory_space=pltpu.HBM)] * 6,
        out_specs=pl.BlockSpec(memory_space=pltpu.VMEM),
        scratch_shapes=[
            pltpu.SMEM(block_order.shape, jnp.int32),
            pltpu.VMEM((rows, queries.shape[1] + 2 * new_block_keys.shape[1]), BF16),
            pltpu.VMEM((n_head, lines, HEAD_WIDTH), BF16),
            pltpu.VMEM((n_head, lines, HEAD_WIDTH), BF16),
            pltpu.VMEM((n // 2, lines, HEAD_WIDTH), BF16),
            pltpu.VMEM((2, total_keys, width), BF16),
            pltpu.VMEM((width, total_keys), BF16),
            pltpu.VMEM((n_head, 2, TILE, width), BF16),
            pltpu.VMEM((n // 2, lines + STAT_ROWS, HEAD_WIDTH), BF16),
            pltpu.VMEM((n // 2, lines + STAT_ROWS, HEAD_WIDTH), BF16),
            dma((2,)),
            dma((4,)),
            dma((2,)),
        ],
        compiler_params=pltpu.CompilerParams(
            collective_id=0, has_side_effects=True, vmem_limit_bytes=48 * 1024 * 1024
        ),
    )(
        stretch_start,
        *[
            pltpu.with_memory_space_constraint(x, pltpu.HBM)
            for x in (
                block_order,
                queries,
                new_block_keys,
                new_block_values,
                stored_keys,
                stored_values,
            )
        ],
    )


def solution(mesh):
    return jax.shard_map(
        functools.partial(on_device, mesh.shape["ctx"], mesh.shape["head"]),
        mesh=mesh,
        in_specs=(
            P(("ctx", "head"), None),
            P(("ctx", "head"), None),
            P(("ctx", "head"), None),
            P("ctx", "head"),
            P("ctx", "head"),
            P(),
            P(),
        ),
        out_specs=P(("ctx", "head"), None),
        check_vma=False,
    )
```

```python
import functools
import math

import jax
import jax.numpy as jnp
from jax import lax
from jax.experimental import pallas as pl
from jax.experimental.pallas import tpu as pltpu
from jax.sharding import PartitionSpec as P

QUERY_HEADS = 16
HEAD_WIDTH = 128
NEG_FILL = -1e30
FAR = 2**30
TILE = 16
PAIR = 2
STAT_ROWS = 2
SCALE = 1.0 / math.sqrt(HEAD_WIDTH)
SCALE2 = SCALE * math.log2(math.e)
MESH = pl.DeviceIdType.MESH
F32 = jnp.float32
BF16 = jnp.bfloat16


def each(first, count, body):
    if count - first <= 64:
        for step in range(first, count):
            body(step)
    else:
        lax.fori_loop(first, count, lambda step, _: body(step), None)


def chunk_of(count):
    return max(c for c in range(1, 33) if count % c == 0)


def kernel(
    n_ctx,
    n_head,
    stretch_ref,
    order_hbm,
    q_hbm,
    nk_hbm,
    nv_hbm,
    k_hbm,
    v_hbm,
    out_ref,
    order_ref,
    stage,
    qsend,
    carry,
    qrecv,
    kv,
    kt,
    fresh,
    osend,
    orecv,
    local_sem,
    q_sems,
    kv_sems,
    o_sems,
):
    n = n_ctx * n_head
    rows = q_hbm.shape[0]
    cache, width = k_hbm.shape
    kv_heads = width // HEAD_WIDTH
    heads = QUERY_HEADS // n_head
    lines = heads * rows
    kv_lines = lines // kv_heads
    half = rows * n_head // 2
    per_half = half // rows
    crew = PAIR * n_head
    servers = n // 2
    plane = n_ctx // 4
    early = plane * n_head
    old_keys = cache * PAIR
    total_keys = kv.shape[1]
    ctx = lax.axis_index("ctx")
    head = lax.axis_index("head")
    me = ctx * n_head + head
    core = lax.rem(ctx, PAIR)
    lead = ctx - core
    seat = core * n_head + head
    desk = (ctx // PAIR) * n_head + head
    spot = lax.rem(me, servers)
    is_odd = core == 1
    is_low = ctx < 2 * plane
    is_early = ctx < plane
    is_relay = jnp.logical_not(is_early) & is_low
    origin_ctx = ctx - plane + 1 - 2 * core
    own = jnp.where(is_low, core, 1 - core) == 1
    first_client = jnp.where(is_odd, 0, servers)

    def place(slot):
        return (slot // n_head, lax.rem(slot, n_head))

    def server_at(index):
        pair, h = place(index)
        return (pair * PAIR + jnp.where(is_low, 1, 0), h)

    def remote(source, target, send, recv, to):
        return pltpu.make_async_remote_copy(
            src_ref=source,
            dst_ref=target,
            send_sem=send,
            recv_sem=recv,
            device_id=to,
            device_id_type=MESH,
        )

    barrier = pltpu.get_barrier_semaphore()

    def signal(to):
        pl.semaphore_signal(barrier, inc=1, device_id=to, device_id_type=MESH)

    def greet(slot):
        @pl.when(slot != me)
        def _():
            signal(place(slot))

    @pl.when(is_odd)
    def _():
        each(0, early, lambda i: greet(early + lax.rem(me + i, early)))

    @pl.when(jnp.logical_not(is_odd))
    def _():
        each(0, servers, lambda i: greet(servers + lax.rem(me + i, servers)))

    @pl.when(is_relay)
    def _():
        signal((origin_ctx, head))

    for step in range(1, crew):
        c, h = place(lax.rem(seat + step, crew))
        signal((lead + c, h))

    own_rows = pl.ds(pl.multiple_of(core * cache, TILE), cache)
    q_width = q_hbm.shape[1]
    new_width = nk_hbm.shape[1]
    at = 0
    for source in (q_hbm, nk_hbm, nv_hbm):
        wide = source.shape[1]
        pltpu.make_async_copy(source, stage.at[:, at : at + wide], local_sem.at[0]).start()
        at += wide
    order_load = pltpu.make_async_copy(order_hbm, order_ref, local_sem.at[1])
    order_load.start()
    for t, source in enumerate((k_hbm, v_hbm)):
        pltpu.make_async_copy(source, kv.at[t, own_rows], local_sem.at[2]).start()

    pltpu.make_async_copy(stage, stage, local_sem.at[0]).wait()
    block = stage[:, :q_width].astype(F32)
    for h in range(n_head):
        pieces = [
            block[:, (h * heads + i) * HEAD_WIDTH : (h * heads + i + 1) * HEAD_WIDTH]
            for i in range(heads)
        ]
        qsend[h] = jnp.concatenate(pieces, axis=0).astype(BF16)
    blank = jnp.zeros((TILE - rows, width), F32)
    for t in range(2):
        new = stage[:, q_width + t * new_width : q_width + (t + 1) * new_width].astype(F32)
        for h in range(n_head):
            part = new[:, h * width : (h + 1) * width]
            fresh[h, t] = jnp.concatenate([part, blank], axis=0).astype(BF16)

    @pl.when(is_early)
    def _():
        pl.semaphore_wait(barrier, crew)

    @pl.when(jnp.logical_not(is_early) & own)
    def _():
        pl.semaphore_wait(barrier, servers - 1 + crew - 1)

    @pl.when(jnp.logical_not(is_early | own))
    def _():
        pl.semaphore_wait(barrier, servers + crew - 1)

    wave = jnp.where(spot >= early, 1, 0)

    @pl.when(is_early)
    def _():
        remote(qsend, carry, q_sems.at[3], q_sems.at[2], (ctx + plane + 1 - 2 * core, head)).start()

    @pl.when(is_relay)
    def _():
        remote(qsend, carry, q_sems.at[3], q_sems.at[2], (ctx, head)).wait_recv()

        def pass_on(step):
            to = servers - 1 - step
            stays = (to == desk) & is_odd
            returns = (to == origin_ctx // PAIR * n_head + head) & (
                lax.rem(origin_ctx, PAIR) == 1
            )

            @pl.when(jnp.logical_not(stays | returns))
            def _():
                to_ctx, to_head = server_at(to)
                remote(
                    carry.at[to_head],
                    qrecv.at[origin_ctx * n_head + head],
                    q_sems.at[3],
                    q_sems.at[0],
                    (to_ctx, to_head),
                ).start()

        each(0, servers, pass_on)

        @pl.when(is_odd)
        def _():
            qrecv[origin_ctx * n_head + head] = carry[head]

    def new_rows(seat):
        return pl.ds(pl.multiple_of(old_keys + TILE * seat, TILE), TILE)

    for t, source in enumerate((k_hbm, v_hbm)):
        remote(
            source, kv.at[t, own_rows], kv_sems.at[0], kv_sems.at[1], (lead + 1 - core, head)
        ).start()
    for step in range(1, crew):
        to_core, to_head = place(lax.rem(seat + step, crew))
        remote(
            fresh.at[to_head],
            kv.at[:, new_rows(seat)],
            kv_sems.at[0],
            kv_sems.at[1],
            (lead + to_core, to_head),
        ).start()

    def send_queries(step):
        to = lax.rem(desk + servers - step, servers)

        @pl.when(jnp.logical_not(own & (to == desk)))
        def _():
            to_ctx, to_head = server_at(to)
            remote(
                qsend.at[to_head],
                qrecv.at[spot],
                q_sems.at[3],
                q_sems.at[wave],
                (to_ctx, to_head),
            ).start()

    @pl.when(jnp.logical_not(is_early))
    def _():
        each(1, servers + 1, send_queries)

    @pl.when(own)
    def _():
        qrecv[spot] = qsend[head]

    kv[:, new_rows(seat)] = fresh[head]
    spare = total_keys - old_keys - TILE * crew
    if spare:
        for t in range(2):
            kv[t, total_keys - spare :] = jnp.zeros((spare, width), BF16)

    order_load.wait()
    loaded = kv.at[:, own_rows]
    pltpu.make_async_copy(loaded, loaded, local_sem.at[2]).wait()

    def start_of(slot):
        return order_ref[slot // per_half] * half + lax.rem(slot, per_half) * rows

    split = (old_keys // 128) * 128
    column = lax.broadcasted_iota(jnp.int32, (1, total_keys), 1)
    cached = (column < old_keys) & (column + lead * cache < stretch_ref[0])
    key_pos = jnp.where(cached, -1, FAR)
    for j in range(crew):
        offset = column - (old_keys + TILE * j)
        pos = start_of(lead * n_head + j) + offset
        key_pos = jnp.where((offset >= 0) & (offset < rows), pos, key_pos)

    here = (ctx, head)
    bulk = kv.at[:, pl.ds(0, cache + TILE * (crew - 1))]
    remote(bulk, bulk, kv_sems.at[0], kv_sems.at[1], here).wait()
    kt[...] = kv[0].T

    def expect(index, less, count):
        def wait_for(slots):
            block = qrecv.at[pl.ds(0, slots)]
            remote(block, block, q_sems.at[3], q_sems.at[index], here).wait_recv()

        @pl.when(less)
        def _():
            wait_for(count - 1)

        @pl.when(jnp.logical_not(less))
        def _():
            wait_for(count)

    def attend(first, group):
        size = group * kv_lines
        block = qrecv[pl.ds(first, group)].astype(F32)
        tail = total_keys - split
        query_pos = jnp.concatenate(
            [
                jnp.full((kv_lines, tail), start_of(first_client + first + i), jnp.int32)
                for i in range(group)
            ],
            axis=0,
        )
        query_pos = query_pos + lax.rem(
            lax.broadcasted_iota(jnp.int32, (size, tail), 0), rows
        )
        scores = jnp.concatenate(
            [
                lax.dot_general(
                    block[:, g * kv_lines : (g + 1) * kv_lines]
                    .reshape(size, HEAD_WIDTH)
                    .astype(BF16),
                    kt[g * HEAD_WIDTH : (g + 1) * HEAD_WIDTH],
                    (((1,), (0,)), ((), ())),
                    preferred_element_type=F32,
                )
                for g in range(kv_heads)
            ],
            axis=0,
        )
        query_pos = jnp.concatenate([query_pos] * kv_heads, axis=0)
        old = jnp.where(key_pos[:, :split] < 0, scores[:, :split], NEG_FILL)
        new = jnp.where(key_pos[:, split:] <= query_pos, scores[:, split:], NEG_FILL)
        scores = jnp.concatenate([old, new], axis=1)
        peak = jnp.max(scores, axis=1, keepdims=True)
        weights = jnp.exp2((scores - peak) * SCALE2)
        total = jnp.sum(weights, axis=1, keepdims=True)
        sums = lax.dot_general(
            weights.astype(BF16), kv[1], (((1,), (0,)), ((), ())), preferred_element_type=F32
        )
        part = jnp.concatenate(
            [
                sums[g * size : (g + 1) * size, g * HEAD_WIDTH : (g + 1) * HEAD_WIDTH]
                for g in range(kv_heads)
            ],
            axis=0,
        )
        part = part / total
        mass = peak * SCALE + jnp.log(total)
        high = mass.astype(BF16).astype(F32)
        rest = mass - high
        mid = rest.astype(BF16).astype(F32)
        low = rest - mid
        lane = lax.broadcasted_iota(jnp.int32, (kv_heads * size, HEAD_WIDTH), 1)
        row = lax.broadcasted_iota(jnp.int32, (kv_heads * size, HEAD_WIDTH), 0)
        line = lax.rem(row, kv_lines) + kv_lines * (row // size)
        stat = jnp.where(lane < lines, high, jnp.where(lane < 2 * lines, mid, low))
        stat = jnp.where((lane < 3 * lines) & (lax.rem(lane, lines) == line), stat, 0.0)
        stat = stat.reshape(kv_heads, group, kv_lines, HEAD_WIDTH)
        stat = jnp.sum(jnp.sum(stat, axis=2, keepdims=True), axis=0)
        parts = [
            part[g * size : (g + 1) * size].reshape(group, kv_lines, HEAD_WIDTH)
            for g in range(kv_heads)
        ]
        osend[pl.ds(first, group), 0:lines] = jnp.concatenate(parts, axis=1).astype(BF16)
        osend[pl.ds(first, group), lines : lines + STAT_ROWS] = jnp.broadcast_to(
            stat, (group, STAT_ROWS, HEAD_WIDTH)
        ).astype(BF16)

    is_far = jnp.where(ctx >= 3 * plane, 1, 0)

    def send_part(index):
        slot = first_client + index

        @pl.when(slot != me)
        def _():
            remote(
                osend.at[index], orecv.at[desk], o_sems.at[0], o_sems.at[1 + is_far], place(slot)
            ).start()

    for index, first, last in ((0, 0, early), (1, early, servers)):
        less = own & (wave == index)
        if index == 0:
            less = less | (own & is_relay)
        count = last - first
        expect(index, less, count)
        group = chunk_of(count)
        each(0, count // group, lambda i: attend(first + i * group, group))
        each(first, last, send_part)

    @pl.when(own)
    def _():
        orecv[desk] = osend[spot]

    def sent(sem, blocks):
        block = qrecv.at[pl.ds(0, blocks)]
        remote(block, block, sem, q_sems.at[0], here).wait_send()

    @pl.when(is_early)
    def _():
        sent(q_sems.at[3], n_head)

    @pl.when(is_relay & own)
    def _():
        sent(q_sems.at[3], servers - 1)
        sent(q_sems.at[3], servers - 1)

    @pl.when(is_relay & jnp.logical_not(own))
    def _():
        sent(q_sems.at[3], servers)
        sent(q_sems.at[3], servers - 1)

    @pl.when(jnp.logical_not(is_low) & own)
    def _():
        sent(q_sems.at[3], servers - 1)

    @pl.when(jnp.logical_not(is_low | own))
    def _():
        sent(q_sems.at[3], servers)

    def answers(count, which=1):
        block = orecv.at[pl.ds(0, count)]
        return remote(block, block, o_sems.at[0], o_sems.at[which], here)

    lane = lax.broadcasted_iota(jnp.int32, (lines, HEAD_WIDTH), 1)
    line = lax.broadcasted_iota(jnp.int32, (lines, HEAD_WIDTH), 0)
    diagonal = (lane < 3 * lines) & (lax.rem(lane, lines) == line)
    sums = [None] * n_head
    for which, first, last in ((1, 0, 3 * early // 2), (2, 3 * early // 2, servers)):
        count = last - first
        less = own & (is_far == which - 1)

        @pl.when(less)
        def _():
            answers(count - 1, which).wait_recv()

        @pl.when(jnp.logical_not(less))
        def _():
            answers(count, which).wait_recv()

        block = orecv[first:last].astype(F32)
        block = block.reshape(count // n_head, n_head, lines + STAT_ROWS, HEAD_WIDTH)
        for h in range(n_head):
            spread = jnp.where(diagonal[None], block[:, h, lines : lines + 1], 0.0)
            mass = jnp.sum(spread, axis=2, keepdims=True)
            top = jnp.max(mass, axis=0, keepdims=True)
            share = jnp.exp(mass - top)
            part = (jnp.sum(share * block[:, h, :lines], axis=0), jnp.sum(share, axis=0), top[0])
            if sums[h] is None:
                sums[h] = part
            else:
                top = jnp.maximum(sums[h][2], part[2])
                left, right = jnp.exp(sums[h][2] - top), jnp.exp(part[2] - top)
                result = (sums[h][0] * left + part[0] * right) / (
                    sums[h][1] * left + part[1] * right
                )
                for i in range(heads):
                    at = (h * heads + i) * HEAD_WIDTH
                    out_ref[:, at : at + HEAD_WIDTH] = result[i * rows : (i + 1) * rows].astype(BF16)

    @pl.when(own)
    def _():
        answers(servers - 1).wait_send()

    @pl.when(jnp.logical_not(own))
    def _():
        answers(servers).wait_send()


def on_device(
    n_ctx,
    n_head,
    queries,
    new_block_keys,
    new_block_values,
    stored_keys,
    stored_values,
    stretch_start,
    block_order,
):
    n = n_ctx * n_head
    rows = queries.shape[0]
    cache, width = stored_keys.shape
    crew = PAIR * n_head
    lines = QUERY_HEADS // n_head * rows
    total_keys = cache * PAIR + TILE * crew
    total_keys = (total_keys + 127) // 128 * 128
    dma = pltpu.SemaphoreType.DMA
    return pl.pallas_call(
        functools.partial(kernel, n_ctx, n_head),
        out_shape=jax.ShapeDtypeStruct(queries.shape, BF16),
        in_specs=[pl.BlockSpec(memory_space=pltpu.SMEM)]
        + [pl.BlockSpec(memory_space=pltpu.HBM)] * 6,
        out_specs=pl.BlockSpec(memory_space=pltpu.VMEM),
        scratch_shapes=[
            pltpu.SMEM(block_order.shape, jnp.int32),
            pltpu.VMEM((rows, queries.shape[1] + 2 * new_block_keys.shape[1]), BF16),
            pltpu.VMEM((n_head, lines, HEAD_WIDTH), BF16),
            pltpu.VMEM((n_head, lines, HEAD_WIDTH), BF16),
            pltpu.VMEM((n // 2, lines, HEAD_WIDTH), BF16),
            pltpu.VMEM((2, total_keys, width), BF16),
            pltpu.VMEM((width, total_keys), BF16),
            pltpu.VMEM((n_head, 2, TILE, width), BF16),
            pltpu.VMEM((n // 2, lines + STAT_ROWS, HEAD_WIDTH), BF16),
            pltpu.VMEM((n // 2, lines + STAT_ROWS, HEAD_WIDTH), BF16),
            dma((3,)),
            dma((4,)),
            dma((2,)),
            dma((3,)),
        ],
        compiler_params=pltpu.CompilerParams(
            collective_id=0, has_side_effects=True, vmem_limit_bytes=48 * 1024 * 1024
        ),
    )(
        stretch_start,
        *[
            pltpu.with_memory_space_constraint(x, pltpu.HBM)
            for x in (
                block_order,
                queries,
                new_block_keys,
                new_block_values,
                stored_keys,
                stored_values,
            )
        ],
    )


def solution(mesh):
    return jax.shard_map(
        functools.partial(on_device, mesh.shape["ctx"], mesh.shape["head"]),
        mesh=mesh,
        in_specs=(
            P(("ctx", "head"), None),
            P(("ctx", "head"), None),
            P(("ctx", "head"), None),
            P("ctx", "head"),
            P("ctx", "head"),
            P(),
            P(),
        ),
        out_specs=P(("ctx", "head"), None),
        check_vma=False,
    )
```
